256 devices in a mesh: tm: 32 (over y, z_hi, x), head: 8 (over z_lo, core).
Axes of the slice: x: 4, y: 4, z: 8 (z_hi: 2, z_lo: 4; z = z_hi * 4 + z_lo), core: 2. Of those that a mesh axis runs over, the one named last changes fastest.
Arguments:
- clean_qkv: bfloat16 [3, 16384, 5120], P(None, 'tm', 'head'), may hold values from -140 to 140
- noise_qkv: bfloat16 [3, 16384, 5120], P(None, 'tm', 'head'), may hold values from -140 to 140
- timestep: int32 [32], P('tm'), may hold values from 1 to 999
- gain_q: float32 [5120], P('head'), may hold values from 0.1 to 1.9
- gain_k: float32 [5120], P('head'), may hold values from 0.1 to 1.9
- attended_grad: bfloat16 [16384, 5120], P('tm', 'head'), may hold values from -6 to 6
Outputs:
- attended: bfloat16 [16384, 5120], P('tm', 'head')
- clean_grads: float32 [3, 16384, 5120], P(None, 'tm', 'head')
The draws below stay inside these ranges and needn't reach their ends.
All inputs are finite; a program needn't handle non-finite values.
Results may differ from the reference program's by a relative error of at most 0.012.
The reference program's roundings to bfloat16 on the way count: a program that leaves them out, or rounds other values in their place, can miss the bound.
Values may be sent and summed in bfloat16 or wider, within the bound.
No kernel may reach another device: no remote copies, remote signals or barrier semaphores. Data moves between devices by JAX's collectives and lax.ppermute only.
A program may use at most 128 MiB of HBM per device.

```python
import math
import jax
import jax.numpy as jnp
from jax import lax

D = 5120
HEADS = 40
HEAD_DIM = 128
SPAN_ROWS = 512
CONTEXT = 3
SPANS = 32
TOKENS = 16384


def field_draw(key, tag):
    own_key = jax.random.fold_in(key, tag)
    value_key, scale_key = jax.random.split(own_key)
    token_key = jax.random.fold_in(own_key, 7)
    fields = jnp.clip(jax.random.normal(value_key, (3, TOKENS, D), jnp.float32), -6.0, 6.0)
    token_scale = jnp.exp(jax.random.uniform(token_key, (3, TOKENS, 1), jnp.float32) * math.log(10.0))
    head_scale = jnp.exp(jax.random.uniform(scale_key, (3, TOKENS, HEADS), jnp.float32) * math.log(1.2))
    fields = fields * token_scale * jnp.repeat(head_scale, HEAD_DIM, axis=2)
    return fields


def draw_clean_qkv(key, part):
    return field_draw(key, 1).astype(jnp.bfloat16)


def draw_noise_qkv(key, part):
    return field_draw(key, 2).astype(jnp.bfloat16)


def with_ends(drawn, key, least, largest):
    extent = drawn.shape
    spot = [jax.random.randint(jax.random.fold_in(key, axis), (), 0, extent[axis]) for axis in range(len(extent))]
    drawn = drawn.at[tuple(spot)].set(least)
    longest = extent.index(max(extent))
    spot[longest] = (spot[longest] + 1) % extent[longest]
    return drawn.at[tuple(spot)].set(largest)


def block_scale(rng, extent, pieces, smallest, high):
    loudness, own = 1.0, jax.random.fold_in(rng, 6)
    for position, blocks in pieces:
        steps = jnp.exp(jax.random.uniform(jax.random.fold_in(own, position), (blocks,), jnp.float32, smallest / len(pieces), high / len(pieces)))
        loudness = loudness * jnp.repeat(steps, extent[position] // blocks).reshape([-1 if axis == position else 1 for axis in range(len(extent))])
    return loudness


def scatter_about(stream_key, extent, scale, reach, cuts=(), kind=jnp.bfloat16):
    drawn = jax.random.normal(stream_key, extent, jnp.float32) * scale
    if len(cuts) > 0:
        drawn = block_scale(stream_key, extent, cuts, -0.22, 0.18) * drawn
    return jnp.clip(drawn, min=-reach, max=reach).astype(kind)


def setup_inputs(seed: int = 0) -> dict:
    seeds = jax.random.split(jax.random.key(seed), 7)
    return {
        "clean_qkv": draw_clean_qkv(jax.random.fold_in(seeds[6], 71), 0),
        "noise_qkv": draw_noise_qkv(jax.random.fold_in(seeds[6], 71), 0),
        "timestep": with_ends(jax.random.randint(seeds[2], (SPANS,), 1, 1000), jax.random.fold_in(seeds[2], 1), 1, 999).astype(jnp.int32),
        "gain_q": jnp.clip(1.0 + 0.18 * jax.random.normal(seeds[3], (D,), jnp.float32), 0.1, 1.9),
        "gain_k": jnp.clip(1.0 + 0.18 * jax.random.normal(seeds[4], (D,), jnp.float32), 0.1, 1.9),
        "attended_grad": scatter_about(seeds[5], (TOKENS, D), 1.0, 6.0, ((0, 32), (1, 8))),
    }


epsilon = 1e-06
masked_score = -1e+30

def noise_share_of(timestep):
    level = timestep.astype(jnp.float32) / 1000.0
    return 5.0 * level / (1.0 + 4.0 * level)

def inverse_rms(field):
    return lax.rsqrt(lax.optimization_barrier(jnp.mean(field * field, axis=-1, keepdims=True)) + epsilon)

def norm_backward(field, inverse, gain, grad):
    inner = lax.optimization_barrier(jnp.mean(field * gain * grad, axis=-1, keepdims=True))
    return inverse * gain * grad - field * inverse ** 3 * inner

def reference(clean_qkv, noise_qkv, timestep, gain_q, gain_k, attended_grad):
    highest = lax.Precision.HIGHEST
    noise_all = noise_share_of(timestep)
    clean_key_pre = clean_qkv[1].astype(jnp.float32)
    key_clean_all = (clean_key_pre * inverse_rms(clean_key_pre) * gain_k).astype(jnp.bfloat16)
    value_clean_all = clean_qkv[2]
    score_scale = HEAD_DIM ** (-0.5)

    def span_step(carried_state, span_index):
        pending_keys, pending_values = carried_state
        first_row = (span_index * SPAN_ROWS).astype(jnp.int32)
        noise_share = noise_all[span_index]
        keep_share = 1.0 - noise_share
        clean_field = lax.dynamic_slice_in_dim(clean_qkv, first_row, SPAN_ROWS, 1).astype(jnp.float32)
        noise_field = lax.dynamic_slice_in_dim(noise_qkv, first_row, SPAN_ROWS, 1).astype(jnp.float32)
        noisy_field = keep_share * clean_field + noise_share * noise_field
        inverse_query = inverse_rms(noisy_field[0])
        inverse_key = inverse_rms(noisy_field[1])
        inverse_clean = inverse_rms(clean_field[1])
        query_rows = (noisy_field[0] * inverse_query * gain_q).astype(jnp.bfloat16)
        key_own = (noisy_field[1] * inverse_key * gain_k).astype(jnp.bfloat16)
        value_own = noisy_field[2].astype(jnp.bfloat16)
        key_parts = [key_own]
        value_parts = [value_own]
        valid_parts = [jnp.ones((SPAN_ROWS,), dtype=bool)]
        for hop_index in range(1, CONTEXT + 1):
            source_row = (jnp.maximum(span_index - hop_index, 0) * SPAN_ROWS).astype(jnp.int32)
            key_parts.append(lax.dynamic_slice_in_dim(key_clean_all, source_row, SPAN_ROWS, 0))
            value_parts.append(lax.dynamic_slice_in_dim(value_clean_all, source_row, SPAN_ROWS, 0))
            valid_parts.append(jnp.full((SPAN_ROWS,), span_index >= hop_index))
        key_rows = jnp.concatenate(key_parts, axis=0)
        value_rows = jnp.concatenate(value_parts, axis=0)
        key_valid = jnp.concatenate(valid_parts, axis=0)
        query_cube = query_rows.astype(jnp.float32).reshape(SPAN_ROWS, HEADS, HEAD_DIM)
        key_cube = key_rows.astype(jnp.float32).reshape(-1, HEADS, HEAD_DIM)
        value_cube = value_rows.astype(jnp.float32).reshape(-1, HEADS, HEAD_DIM)
        grad_rows = lax.dynamic_slice_in_dim(attended_grad, first_row, SPAN_ROWS, 0)
        grad_cube = grad_rows.astype(jnp.float32).reshape(SPAN_ROWS, HEADS, HEAD_DIM)
        scores = jnp.einsum('qhd,khd->hqk', query_cube, key_cube, precision=highest) * score_scale
        scores = jnp.where(key_valid[None, None, :], scores, masked_score)
        row_max = lax.optimization_barrier(jnp.max(scores, axis=-1, keepdims=True))
        exponent = jnp.exp(scores - row_max)
        attention = exponent / lax.optimization_barrier(jnp.sum(exponent, axis=-1, keepdims=True))
        weights = lax.optimization_barrier(attention.astype(jnp.bfloat16)).astype(jnp.float32)
        output_rows = jnp.einsum('hqk,khd->qhd', weights, value_cube, precision=highest)
        output_rows = output_rows.reshape(SPAN_ROWS, D).astype(jnp.bfloat16)
        grad_probs = jnp.einsum('qhd,khd->hqk', grad_cube, value_cube, precision=highest)
        row_delta = lax.optimization_barrier(jnp.sum(attention * grad_probs, axis=-1, keepdims=True))
        grad_scores = (attention * (grad_probs - row_delta) * score_scale).astype(jnp.bfloat16)
        grad_scores = lax.optimization_barrier(grad_scores).astype(jnp.float32)
        grad_query = jnp.einsum('hqk,khd->qhd', grad_scores, key_cube, precision=highest).reshape(SPAN_ROWS, D)
        grad_keys = jnp.einsum('hqk,qhd->khd', grad_scores, query_cube, precision=highest).reshape(-1, D)
        grad_values = jnp.einsum('hqk,qhd->khd', weights, grad_cube, precision=highest).reshape(-1, D)
        grad_query_pre = norm_backward(noisy_field[0], inverse_query, gain_q, grad_query)
        grad_own_pre = norm_backward(noisy_field[1], inverse_key, gain_k, grad_keys[:SPAN_ROWS])
        grad_clean_pre = norm_backward(clean_field[1], inverse_clean, gain_k, pending_keys[0])
        clean_grads = jnp.stack([keep_share * grad_query_pre, keep_share * grad_own_pre + grad_clean_pre, keep_share * grad_values[:SPAN_ROWS] + pending_values[0]])
        next_keys = []
        next_values = []
        for hop_index in range(CONTEXT - 1):
            lower = (hop_index + 1) * SPAN_ROWS
            next_keys.append(pending_keys[hop_index + 1] + grad_keys[lower:lower + SPAN_ROWS])
            next_values.append(pending_values[hop_index + 1] + grad_values[lower:lower + SPAN_ROWS])
        next_keys.append(grad_keys[CONTEXT * SPAN_ROWS:])
        next_values.append(grad_values[CONTEXT * SPAN_ROWS:])
        return ((jnp.stack(next_keys), jnp.stack(next_values)), (output_rows, clean_grads))
    start_state = (jnp.zeros((CONTEXT, SPAN_ROWS, D), jnp.float32), jnp.zeros((CONTEXT, SPAN_ROWS, D), jnp.float32))
    final_state, results = lax.scan(span_step, start_state, jnp.arange(SPANS, dtype=jnp.int32), reverse=True)
    outputs, gradients = results
    attended = outputs.reshape(TOKENS, D)
    clean_grads = jnp.transpose(gradients, (1, 0, 2, 3)).reshape(3, TOKENS, D)
    return (attended, clean_grads)
```

```python
import math

import jax
import jax.numpy as jnp
from jax import lax
from jax.experimental import pallas as pl
from jax.experimental.pallas import tpu as pltpu
from jax.sharding import PartitionSpec as P

D = 5120
HEAD_DIM = 128
CONTEXT = 3
COLUMNS = 4
HEAD_CHUNKS = (2, 2, 1)
KEY_TILE = 256

epsilon = 1e-06
masked_score = -1e30
NT = (((1,), (1,)), ((), ()))
NN = (((1,), (0,)), ((), ()))


def dot(left, right, dims):
    return lax.dot_general(left, right, dims, preferred_element_type=jnp.float32)


def noise_share_of(timestep):
    level = timestep.astype(jnp.float32) / 1000.0
    return 5.0 * level / (1.0 + 4.0 * level)


def shift_spans(block, distance, columns=range(COLUMNS)):
    count = lax.axis_size("tm")
    route = [
        (i, i + distance)
        for i in range(count)
        if 0 <= i + distance < count and i % COLUMNS in columns
    ]
    return lax.ppermute(block, "tm", route)


def shift_columns(block, distance, kind):
    count = lax.axis_size("tm")
    route = []
    for i in range(count):
        row, column = divmod(i, COLUMNS)
        target = column + distance
        inside = 0 <= target < COLUMNS
        if kind == "both" or inside == (kind == "inside"):
            route.append((i, row * COLUMNS + target % COLUMNS))
    return lax.ppermute(block, "tm", route)


def attention_body(
    flags, cols, gain, query, key_own, value_own, grad,
    own_1, own_2, own_3, wrap_1, wrap_2, wrap_3, *refs
):
    (attended, grad_query, grad_key, grad_value, back_1, back_2, back_3, inner,
     exps, probs, keys, values) = refs[-12:]
    rows = query.shape[0]
    scale = HEAD_DIM**-0.5
    exponent_scale = scale * math.log2(math.e)
    gains = gain[...]
    sources = ((own_1, wrap_1), (own_2, wrap_2), (own_3, wrap_3))
    backs = (back_1, back_2, back_3)

    @pl.when(pl.program_id(0) == 0)
    def _():
        inner[...] = jnp.zeros_like(inner)

    keys[0:rows] = key_own[...]
    values[0:rows] = value_own[...]
    for hop, (own, wrap) in enumerate(sources):
        inside = flags[hop] > 0
        block = pl.ds((hop + 1) * rows, rows)
        raw = jnp.where(inside, own[0], wrap[0]).astype(jnp.float32)
        keys[block] = (raw * cols[:, hop : hop + 1] * gains).astype(jnp.bfloat16)
        values[block] = jnp.where(inside, own[1], wrap[1])
    queries = query[...]
    grads = grad[...]
    tiles = rows // KEY_TILE

    row_max = None
    for block in range(CONTEXT + 1):
        block_max = None
        for tile in range(tiles):
            part = pl.ds(block * rows + tile * KEY_TILE, KEY_TILE)
            scores = dot(keys[part], queries, NT)
            exps[part] = scores
            tile_max = jnp.max(scores, axis=0, keepdims=True)
            block_max = tile_max if block_max is None else jnp.maximum(block_max, tile_max)
        if block > 0:
            block_max = jnp.where(flags[2 + block] > 0, block_max, masked_score)
        row_max = block_max if row_max is None else jnp.maximum(row_max, block_max)
    offset = row_max * exponent_scale
    total = jnp.zeros((1, rows), jnp.float32)
    delta = jnp.zeros((1, rows), jnp.float32)
    for block in range(CONTEXT + 1):
        block_offset = offset
        if block > 0:
            block_offset = jnp.where(flags[2 + block] > 0, offset, -masked_score)
        for tile in range(tiles):
            part = pl.ds(block * rows + tile * KEY_TILE, KEY_TILE)
            exponent = jnp.exp2(exps[part] * exponent_scale - block_offset)
            grad_probs = dot(values[part], grads, NT)
            exps[part] = exponent
            probs[part] = grad_probs
            total = total + jnp.sum(exponent, axis=0, keepdims=True)
            delta = delta + jnp.sum(exponent * grad_probs, axis=0, keepdims=True)
    inverse_total = 1.0 / total
    delta = delta * inverse_total
    output = jnp.zeros((HEAD_DIM, rows), jnp.float32)
    query_grad = jnp.zeros((HEAD_DIM, rows), jnp.float32)
    lane = lax.broadcasted_iota(jnp.int32, (KEY_TILE, 8), 1)
    for block in range(CONTEXT + 1):
        for tile in range(tiles):
            part = pl.ds(block * rows + tile * KEY_TILE, KEY_TILE)
            here = pl.ds(tile * KEY_TILE, KEY_TILE)
            attention = exps[part] * inverse_total
            weights = attention.astype(jnp.bfloat16)
            grad_scores = (attention * (probs[part] - delta) * scale).astype(jnp.bfloat16)
            output = output + dot(values[part].T, weights, NN)
            query_grad = query_grad + dot(keys[part].T, grad_scores, NN)
            value_part = dot(weights, grads, NN)
            key_part = dot(grad_scores, queries, NN)
            if block == 0:
                grad_key[here] = key_part
                grad_value[here] = value_part
            else:
                back = backs[block - 1]
                back[0, here] = key_part.astype(jnp.bfloat16)
                back[1, here] = value_part.astype(jnp.bfloat16)
                own, wrap = sources[block - 1]
                raw = jnp.where(flags[block - 1] > 0, own[0, here], wrap[0, here])
                product = raw.astype(jnp.float32) * gains * key_part
                inner[here] += jnp.where(
                    lane == block - 1, jnp.sum(product, axis=1, keepdims=True), 0.0
                )
    attended[...] = output.T.astype(jnp.bfloat16)
    grad_query[...] = query_grad.T


def attention_chunk(first, heads, flags, cols, gain, rows_in, own, wrap, previous):
    rows, width = rows_in[0].shape
    here = lambda h: (0, first + h)
    f32, bf16 = jnp.float32, jnp.bfloat16
    wide = pl.BlockSpec((rows, HEAD_DIM), here)
    wide_pair = pl.BlockSpec((2, rows, HEAD_DIM), lambda h: (0, 0, first + h))
    pair = pl.BlockSpec((2, rows, HEAD_DIM), lambda h: (0, 0, h))
    in_specs = (
        [
            pl.BlockSpec(memory_space=pltpu.SMEM),
            pl.BlockSpec(cols.shape, lambda h: (0, 0)),
            pl.BlockSpec((1, HEAD_DIM), here),
        ]
        + [wide] * 4
        + [wide_pair] * 3
        + [pair] * 3
    )
    operands = [flags, cols, gain, *rows_in, *own, *wrap]
    aliases = {}
    for position, array in enumerate(previous):
        aliases[len(operands)] = position
        operands.append(array)
        in_specs.append(pl.BlockSpec(memory_space=pl.ANY))
    back = jax.ShapeDtypeStruct((2, rows, heads * HEAD_DIM), bf16)
    keys = (CONTEXT + 1) * rows
    flops = 6 * 2 * rows * keys * HEAD_DIM * heads
    return pl.pallas_call(
        attention_body,
        grid=(heads,),
        in_specs=in_specs,
        out_specs=[wide] * 4 + [pair] * 3 + [pl.BlockSpec((rows, 8), lambda h: (0, 0))],
        out_shape=[
            jax.ShapeDtypeStruct((rows, width), bf16),
            jax.ShapeDtypeStruct((rows, width), f32),
            jax.ShapeDtypeStruct((rows, width), f32),
            jax.ShapeDtypeStruct((rows, width), f32),
            back,
            back,
            back,
            jax.ShapeDtypeStruct((rows, 8), f32),
        ],
        scratch_shapes=[
            pltpu.VMEM((keys, rows), f32),
            pltpu.VMEM((keys, rows), f32),
            pltpu.VMEM((keys, HEAD_DIM), bf16),
            pltpu.VMEM((keys, HEAD_DIM), bf16),
        ],
        input_output_aliases=aliases,
        compiler_params=pltpu.CompilerParams(
            dimension_semantics=("arbitrary",), vmem_limit_bytes=40 * 2**20
        ),
        cost_estimate=pl.CostEstimate(
            flops=flops, bytes_accessed=heads * 4 * 2**20, transcendentals=rows * keys * heads
        ),
    )(*operands)


def finish_body(
    flags, keep_ref, cols, gain_q, gain_k, clean, noise, grad_query, grad_key, grad_value,
    in_1, in_2, in_3, crossed, *refs
):
    out = refs[-1]
    keep = keep_ref[0]
    share = keep_ref[1]
    f32 = jnp.float32
    clean_key = clean[1].astype(f32)
    noisy_query = keep * clean[0].astype(f32) + share * noise[0].astype(f32)
    noisy_key = keep * clean_key + share * noise[1].astype(f32)
    key_grad = crossed[0].astype(f32)
    value_grad = crossed[1].astype(f32)
    for hop, received in enumerate((in_1, in_2, in_3)):
        inside = flags[6 + hop] > 0
        key_grad = key_grad + jnp.where(inside, received[0], 0).astype(f32)
        value_grad = value_grad + jnp.where(inside, received[1], 0).astype(f32)
    col = lambda i: cols[:, i : i + 1]
    gk = gain_k[...]
    out[0] = keep * (col(0) * gain_q[...] * grad_query[...] - noisy_query * col(3))
    own = col(1) * gk * grad_key[...] - noisy_key * col(4)
    out[1] = keep * own + (col(2) * gk * key_grad - clean_key * col(5))
    out[2] = keep * grad_value[...] + value_grad


def finish_chunk(first, heads, flags, keep, cols, gains, fields, grads, received, crossed, previous):
    _, rows, width = fields[0].shape
    here = lambda h: (0, first + h)
    wide = pl.BlockSpec((rows, HEAD_DIM), here)
    gain_spec = pl.BlockSpec((1, HEAD_DIM), here)
    two = pl.BlockSpec((2, rows, HEAD_DIM), lambda h: (0, 0, first + h))
    pair = pl.BlockSpec((2, rows, HEAD_DIM), lambda h: (0, 0, h))
    smem = pl.BlockSpec(memory_space=pltpu.SMEM)
    operands = [flags, keep, cols, *gains, *fields, *grads, *received, crossed]
    in_specs = (
        [smem, smem, pl.BlockSpec(cols.shape, lambda h: (0, 0))]
        + [gain_spec] * 2
        + [two] * 2
        + [wide] * 3
        + [pair] * 4
    )
    aliases = {}
    if previous is not None:
        aliases[len(operands)] = 0
        operands.append(previous)
        in_specs.append(pl.BlockSpec(memory_space=pl.ANY))
    return pl.pallas_call(
        finish_body,
        grid=(heads,),
        in_specs=in_specs,
        out_specs=pl.BlockSpec((3, rows, HEAD_DIM), lambda h: (0, 0, first + h)),
        out_shape=jax.ShapeDtypeStruct((3, rows, width), jnp.float32),
        input_output_aliases=aliases,
        compiler_params=pltpu.CompilerParams(dimension_semantics=("arbitrary",)),
        cost_estimate=pl.CostEstimate(
            flops=rows * HEAD_DIM * heads * 30,
            bytes_accessed=heads * rows * HEAD_DIM * 48,
            transcendentals=0,
        ),
    )(*operands)


def on_device(clean_qkv, noise_qkv, timestep, gain_q, gain_k, attended_grad):
    f32, bf16 = jnp.float32, jnp.bfloat16
    span = lax.axis_index("tm")
    column = span % COLUMNS
    chunks = []
    first = 0
    for heads in HEAD_CHUNKS:
        chunks.append((first, heads))
        first += heads

    def lanes(first, heads):
        return slice(first * HEAD_DIM, (first + heads) * HEAD_DIM)

    context = clean_qkv[1:3]
    crossing = []
    own = None
    for first, heads in chunks:
        crossing.append(
            shift_spans(context[:, :, lanes(first, heads)], COLUMNS, range(1, COLUMNS))
        )
        if own is None:
            own = [shift_columns(context, hop, "inside") for hop in range(1, CONTEXT + 1)]

    noise_share = noise_share_of(timestep[0])
    keep_share = 1.0 - noise_share
    clean_field = clean_qkv.astype(f32)
    noisy_field = keep_share * clean_field + noise_share * noise_qkv.astype(f32)
    squares = jnp.stack(
        [
            jnp.sum(noisy_field[0] * noisy_field[0], axis=-1),
            jnp.sum(noisy_field[1] * noisy_field[1], axis=-1),
            jnp.sum(clean_field[1] * clean_field[1], axis=-1),
        ]
    )
    inverse = lax.rsqrt(lax.psum(squares, "head") / D + epsilon)
    context_inverse = [shift_spans(inverse[2], hop) for hop in range(1, CONTEXT + 1)]
    query_rows = (noisy_field[0] * inverse[0][:, None] * gain_q).astype(bf16)
    key_own = (noisy_field[1] * inverse[1][:, None] * gain_k).astype(bf16)
    value_own = noisy_field[2].astype(bf16)
    rows_in = [query_rows, key_own, value_own, attended_grad]
    inverse_cols = jnp.stack(context_inverse + [jnp.zeros_like(inverse[2])] * 5).T

    hops = jnp.arange(1, CONTEXT + 1, dtype=jnp.int32)
    flags = jnp.concatenate([column >= hops, span >= hops, column + hops < COLUMNS]).astype(
        jnp.int32
    )
    gain_rows = (gain_q[None, :], gain_k[None, :])

    results = ()
    inner = 0.0
    received = []
    crossed = []
    for (first, heads), cross in zip(chunks, crossing):
        wrap = [shift_columns(cross, hop, "wrapped") for hop in range(1, CONTEXT + 1)]
        out = attention_chunk(
            first, heads, flags, inverse_cols, gain_rows[1], rows_in, own, wrap, results
        )
        results = out[:4]
        inner = inner + out[7]
        back = [shift_columns(out[4 + hop], -(hop + 1), "both") for hop in range(CONTEXT)]
        forward = jnp.zeros(back[0].shape, f32)
        for hop in range(CONTEXT):
            forward = forward + jnp.where(column + hop + 1 >= COLUMNS, back[hop], 0).astype(f32)
        received.append(back)
        crossed.append(shift_spans(forward.astype(bf16), -COLUMNS, range(1, COLUMNS)))
    attended, grad_query, grad_key, grad_value = results

    sums = jnp.stack(
        [
            jnp.sum(noisy_field[0] * gain_q * grad_query, axis=-1),
            jnp.sum(noisy_field[1] * gain_k * grad_key, axis=-1),
        ]
        + [inner[:, hop] for hop in range(CONTEXT)]
    )
    totals = lax.psum(sums, "head") / D
    clean_inner = sum(shift_spans(totals[2 + hop], -(hop + 1)) for hop in range(CONTEXT))
    cubes = inverse**3 * jnp.stack([totals[0], totals[1], clean_inner])
    finish_cols = jnp.concatenate([inverse, cubes, jnp.zeros_like(inverse[:2])]).T
    keep = jnp.stack([keep_share, noise_share])
    clean_grads = None
    for (first, heads), back, cross in zip(chunks, received, crossed):
        clean_grads = finish_chunk(
            first, heads, flags, keep, finish_cols, gain_rows, (clean_qkv, noise_qkv),
            (grad_query, grad_key, grad_value), back, cross, clean_grads,
        )
    return (attended, clean_grads)


def solution(mesh):
    placed = (
        P(None, "tm", "head"),
        P(None, "tm", "head"),
        P("tm"),
        P("head"),
        P("head"),
        P("tm", "head"),
    )
    return jax.shard_map(
        on_device,
        mesh=mesh,
        in_specs=placed,
        out_specs=(P("tm", "head"), P(None, "tm", "head")),
        check_vma=False,
    )
```

```python
import math

import jax
import jax.numpy as jnp
from jax import lax
from jax.experimental import pallas as pl
from jax.experimental.pallas import tpu as pltpu
from jax.sharding import PartitionSpec as P

D = 5120
HEAD_DIM = 128
CONTEXT = 3
COLUMNS = 4
KEY_TILE = 256
VMEM_LIMIT = 60 * 2**20

epsilon = 1e-06
masked_score = -1e30
NT = (((1,), (1,)), ((), ()))
NN = (((1,), (0,)), ((), ()))


def dot(left, right, dims):
    return lax.dot_general(left, right, dims, preferred_element_type=jnp.float32)


def noise_share_of(timestep):
    level = timestep.astype(jnp.float32) / 1000.0
    return 5.0 * level / (1.0 + 4.0 * level)


def shift_spans(block, distance, columns=range(COLUMNS)):
    count = lax.axis_size("tm")
    route = [
        (i, i + distance)
        for i in range(count)
        if 0 <= i + distance < count and i % COLUMNS in columns
    ]
    return lax.ppermute(block, "tm", route)


def shift_columns(block, distance, kind):
    count = lax.axis_size("tm")
    route = []
    for i in range(count):
        row, column = divmod(i, COLUMNS)
        target = column + distance
        inside = 0 <= target < COLUMNS
        if kind == "both" or inside == (kind == "inside"):
            route.append((i, row * COLUMNS + target % COLUMNS))
    return lax.ppermute(block, "tm", route)


def as_columns(rows_ref):
    rows = rows_ref[...]
    return jnp.concatenate([rows] * (HEAD_DIM // 8), axis=0).T


def prepare_body(shares, clean, noise, sums, columns):
    f32 = jnp.float32
    keep, share = shares[0], shares[1]
    clean_key = clean[1].astype(f32)
    query = keep * clean[0].astype(f32) + share * noise[0].astype(f32)
    key = keep * clean_key + share * noise[1].astype(f32)
    lane = lax.broadcasted_iota(jnp.int32, columns.shape, 1)
    step = jnp.zeros(columns.shape, f32)
    for i, field in enumerate((query, key, clean_key)):
        step = jnp.where(lane == i, jnp.sum(field * field, axis=1, keepdims=True), step)

    @pl.when(pl.program_id(0) == 0)
    def _():
        columns[...] = step

    @pl.when(pl.program_id(0) > 0)
    def _():
        columns[...] += step

    @pl.when(pl.program_id(0) == pl.num_programs(0) - 1)
    def _():
        sums[...] = columns[...].T[0:8]


def prepare(shares, clean, noise):
    _, rows, width = clean.shape
    pair = pl.BlockSpec((2, rows, HEAD_DIM), lambda h: (0, 0, h))
    return pl.pallas_call(
        prepare_body,
        grid=(width // HEAD_DIM,),
        in_specs=[pl.BlockSpec(memory_space=pltpu.SMEM), pair, pair],
        out_specs=pl.BlockSpec((8, rows), lambda h: (0, 0)),
        out_shape=jax.ShapeDtypeStruct((8, rows), jnp.float32),
        scratch_shapes=[pltpu.VMEM((rows, HEAD_DIM), jnp.float32)],
        compiler_params=pltpu.CompilerParams(
            dimension_semantics=("arbitrary",), vmem_limit_bytes=VMEM_LIMIT
        ),
        cost_estimate=pl.CostEstimate(
            flops=rows * width * 12, bytes_accessed=rows * width * 8, transcendentals=0
        ),
    )(shares, clean, noise)


def attention_body(
    flags, shares, inverse, gain_q, gain_k, clean, noise, grad,
    first_1, first_2, first_3, both_1, both_2, both_3, last_1, last_2, last_3, *refs
):
    (attended, grad_query, grad_key, grad_value, back_1, back_2, back_3, inner,
     exps, probs, keys, values, cols, products) = refs[-14:]
    f32, bf16 = jnp.float32, jnp.bfloat16
    rows = grad.shape[0]
    scale = HEAD_DIM**-0.5
    exponent_scale = scale * math.log2(math.e)
    keep, share = shares[0], shares[1]
    gains_q, gains_k = gain_q[...], gain_k[...]
    sources = (
        (first_1, both_1, last_1),
        (first_2, both_2, last_2),
        (first_3, both_3, last_3),
    )
    backs = (back_1, back_2, back_3)

    @pl.when(pl.program_id(0) == 0)
    def _():
        products[...] = jnp.zeros_like(products)
        cols[...] = as_columns(inverse)

    field_query = keep * clean[0].astype(f32) + share * noise[0].astype(f32)
    field_key = keep * clean[1].astype(f32) + share * noise[1].astype(f32)
    field_value = keep * clean[2].astype(f32) + share * noise[2].astype(f32)
    queries = (field_query * cols[:, 0:1] * gains_q).astype(bf16)
    keys[0:rows] = (field_key * cols[:, 1:2] * gains_k).astype(bf16)
    values[0:rows] = field_value.astype(bf16)
    for hop, (first, both, last) in enumerate(sources):
        inside = flags[hop] > 0
        block = pl.ds((hop + 1) * rows, rows)
        keys[block] = jnp.where(inside, both[...], last[...])
        values[block] = jnp.where(inside, first[...], both[...])
    grads = grad[...]
    tiles = rows // KEY_TILE

    row_max = None
    for block in range(CONTEXT + 1):
        block_max = None
        for tile in range(tiles):
            part = pl.ds(block * rows + tile * KEY_TILE, KEY_TILE)
            scores = dot(keys[part], queries, NT)
            exps[part] = scores
            tile_max = jnp.max(scores, axis=0, keepdims=True)
            block_max = tile_max if block_max is None else jnp.maximum(block_max, tile_max)
        if block > 0:
            block_max = jnp.where(flags[2 + block] > 0, block_max, masked_score)
        row_max = block_max if row_max is None else jnp.maximum(row_max, block_max)
    offset = row_max * exponent_scale
    total = jnp.zeros((1, rows), f32)
    delta = jnp.zeros((1, rows), f32)
    for block in range(CONTEXT + 1):
        block_offset = offset
        if block > 0:
            block_offset = jnp.where(flags[2 + block] > 0, offset, -masked_score)
        for tile in range(tiles):
            part = pl.ds(block * rows + tile * KEY_TILE, KEY_TILE)
            exponent = jnp.exp2(exps[part] * exponent_scale - block_offset)
            grad_probs = dot(values[part], grads, NT)
            exps[part] = exponent
            probs[part] = grad_probs
            total = total + jnp.sum(exponent, axis=0, keepdims=True)
            delta = delta + jnp.sum(exponent * grad_probs, axis=0, keepdims=True)
    inverse_total = 1.0 / total
    delta = delta * inverse_total
    output = jnp.zeros((HEAD_DIM, rows), f32)
    query_grad = jnp.zeros((HEAD_DIM, rows), f32)
    lane = lax.broadcasted_iota(jnp.int32, (KEY_TILE, HEAD_DIM), 1)

    def add_product(here, index, product):
        product = jnp.sum(product, axis=1, keepdims=True)
        products[here] += jnp.where(lane == index, product, 0.0)

    for block in range(CONTEXT + 1):
        for tile in range(tiles):
            part = pl.ds(block * rows + tile * KEY_TILE, KEY_TILE)
            here = pl.ds(tile * KEY_TILE, KEY_TILE)
            attention = exps[part] * inverse_total
            weights = attention.astype(bf16)
            grad_scores = (attention * (probs[part] - delta) * scale).astype(bf16)
            output = output + dot(values[part].T, weights, NN)
            query_grad = query_grad + dot(keys[part].T, grad_scores, NN)
            value_part = dot(weights, grads, NN)
            key_part = dot(grad_scores, queries, NN)
            if block == 0:
                grad_key[here] = key_part
                grad_value[here] = value_part
                field = keep * clean[1, here].astype(f32) + share * noise[1, here].astype(f32)
                add_product(here, 1, field * gains_k * key_part)
            else:
                back = backs[block - 1]
                back[0, here] = key_part.astype(bf16)
                back[1, here] = value_part.astype(bf16)
                add_product(here, 1 + block, keys[part].astype(f32) * key_part)
    attended[...] = output.T.astype(bf16)
    grad_query[...] = query_grad.T
    for tile in range(tiles):
        here = pl.ds(tile * KEY_TILE, KEY_TILE)
        field = keep * clean[0, here].astype(f32) + share * noise[0, here].astype(f32)
        add_product(here, 0, field * gains_q * grad_query[here])

    @pl.when(pl.program_id(0) == pl.num_programs(0) - 1)
    def _():
        inner[...] = products[...].T[0:8]


def attention_chunk(first, heads, flags, shares, inverse, gains, fields, grad, gathered, last, last_at, previous):
    rows, width = grad.shape
    here = lambda h: (0, first + h)
    f32, bf16 = jnp.float32, jnp.bfloat16
    smem = pl.BlockSpec(memory_space=pltpu.SMEM)
    small = pl.BlockSpec((8, rows), lambda h: (0, 0))
    wide = pl.BlockSpec((rows, HEAD_DIM), here)
    gain_spec = pl.BlockSpec((1, HEAD_DIM), here)
    field_spec = pl.BlockSpec((3, rows, HEAD_DIM), lambda h: (0, 0, first + h))
    last_spec = pl.BlockSpec((rows, HEAD_DIM), lambda h: (0, last_at + h))
    pair = pl.BlockSpec((2, rows, HEAD_DIM), lambda h: (0, 0, h))
    in_specs = (
        [smem, smem, small]
        + [gain_spec] * 2
        + [field_spec] * 2
        + [wide] * 7
        + [last_spec] * 3
    )
    operands = [flags, shares, inverse, *gains, *fields, grad, *gathered, *last]
    aliases = {}
    for position, array in enumerate(previous):
        aliases[len(operands)] = position
        operands.append(array)
        in_specs.append(pl.BlockSpec(memory_space=pl.ANY))
    back = jax.ShapeDtypeStruct((2, rows, heads * HEAD_DIM), bf16)
    keys = (CONTEXT + 1) * rows
    flops = 6 * 2 * rows * keys * HEAD_DIM * heads
    return pl.pallas_call(
        attention_body,
        grid=(heads,),
        in_specs=in_specs,
        out_specs=[wide] * 4 + [pair] * 3 + [small],
        out_shape=[
            jax.ShapeDtypeStruct((rows, width), bf16),
            jax.ShapeDtypeStruct((rows, width), f32),
            jax.ShapeDtypeStruct((rows, width), f32),
            jax.ShapeDtypeStruct((rows, width), f32),
            back,
            back,
            back,
            jax.ShapeDtypeStruct((8, rows), f32),
        ],
        scratch_shapes=[
            pltpu.VMEM((keys, rows), f32),
            pltpu.VMEM((keys, rows), f32),
            pltpu.VMEM((keys, HEAD_DIM), bf16),
            pltpu.VMEM((keys, HEAD_DIM), bf16),
            pltpu.VMEM((rows, HEAD_DIM), f32),
            pltpu.VMEM((rows, HEAD_DIM), f32),
        ],
        input_output_aliases=aliases,
        compiler_params=pltpu.CompilerParams(
            dimension_semantics=("arbitrary",), vmem_limit_bytes=VMEM_LIMIT
        ),
        cost_estimate=pl.CostEstimate(
            flops=flops, bytes_accessed=heads * 4 * 2**20, transcendentals=rows * keys * heads
        ),
    )(*operands)


def finish_body(
    flags, shares, rows_ref, gain_q, gain_k, clean, noise, grad_query, grad_key, grad_value,
    in_1, in_2, in_3, crossed, *refs
):
    out, cols = refs[-2:]
    f32 = jnp.float32
    keep, share = shares[0], shares[1]

    @pl.when(pl.program_id(0) == 0)
    def _():
        cols[...] = as_columns(rows_ref)

    clean_key = clean[1].astype(f32)
    noisy_query = keep * clean[0].astype(f32) + share * noise[0].astype(f32)
    noisy_key = keep * clean_key + share * noise[1].astype(f32)
    key_grad = crossed[0].astype(f32)
    value_grad = crossed[1].astype(f32)
    for hop, received in enumerate((in_1, in_2, in_3)):
        inside = flags[6 + hop] > 0
        key_grad = key_grad + jnp.where(inside, received[0], 0).astype(f32)
        value_grad = value_grad + jnp.where(inside, received[1], 0).astype(f32)
    col = lambda i: cols[:, i : i + 1]
    gk = gain_k[...]
    out[0] = keep * (col(0) * gain_q[...] * grad_query[...] - noisy_query * col(3))
    own = col(1) * gk * grad_key[...] - noisy_key * col(4)
    out[1] = keep * own + (col(2) * gk * key_grad - clean_key * col(5))
    out[2] = keep * grad_value[...] + value_grad


def finish_chunk(first, heads, flags, shares, factors, gains, fields, grads, received, crossed, previous):
    _, rows, width = fields[0].shape
    here = lambda h: (0, first + h)
    wide = pl.BlockSpec((rows, HEAD_DIM), here)
    gain_spec = pl.BlockSpec((1, HEAD_DIM), here)
    two = pl.BlockSpec((2, rows, HEAD_DIM), lambda h: (0, 0, first + h))
    pair = pl.BlockSpec((2, rows, HEAD_DIM), lambda h: (0, 0, h))
    smem = pl.BlockSpec(memory_space=pltpu.SMEM)
    operands = [flags, shares, factors, *gains, *fields, *grads, *received, crossed]
    in_specs = (
        [smem, smem, pl.BlockSpec((8, rows), lambda h: (0, 0))]
        + [gain_spec] * 2
        + [two] * 2
        + [wide] * 3
        + [pair] * 4
    )
    aliases = {}
    if previous is not None:
        aliases[len(operands)] = 0
        operands.append(previous)
        in_specs.append(pl.BlockSpec(memory_space=pl.ANY))
    return pl.pallas_call(
        finish_body,
        grid=(heads,),
        in_specs=in_specs,
        out_specs=pl.BlockSpec((3, rows, HEAD_DIM), lambda h: (0, 0, first + h)),
        out_shape=jax.ShapeDtypeStruct((3, rows, width), jnp.float32),
        scratch_shapes=[pltpu.VMEM((rows, HEAD_DIM), jnp.float32)],
        input_output_aliases=aliases,
        compiler_params=pltpu.CompilerParams(
            dimension_semantics=("arbitrary",), vmem_limit_bytes=VMEM_LIMIT
        ),
        cost_estimate=pl.CostEstimate(
            flops=rows * HEAD_DIM * heads * 30,
            bytes_accessed=heads * rows * HEAD_DIM * 48,
            transcendentals=0,
        ),
    )(*operands)


def head_sum(block):
    count = lax.axis_size("head")
    distance = 1
    while distance < count:
        route = [(i, i ^ distance) for i in range(count)]
        block = block + lax.ppermute(block, "head", route)
        distance *= 2
    return block


def after(value, *earlier):
    return lax.optimization_barrier((value, *earlier))[0]


def on_device(clean_qkv, noise_qkv, timestep, gain_q, gain_k, attended_grad):
    f32, bf16 = jnp.float32, jnp.bfloat16
    span = lax.axis_index("tm")
    column = span % COLUMNS
    steps = range(1, CONTEXT + 1)
    crossers = range(1, COLUMNS)
    value_clean = clean_qkv[2]

    def lanes(block, first, heads):
        return block[:, first * HEAD_DIM : (first + heads) * HEAD_DIM]

    def mixed(own, wrap):
        return [
            shift_columns(jnp.where(column + hop < COLUMNS, own, wrap), hop, "both")
            for hop in steps
        ]

    cross_values = shift_spans(value_clean, COLUMNS, crossers)
    first = [shift_columns(value_clean, hop, "inside") for hop in steps]

    noise_share = noise_share_of(timestep[0])
    shares = jnp.stack([1.0 - noise_share, noise_share])
    squares = prepare(shares, clean_qkv, noise_qkv)
    inverse = lax.rsqrt(head_sum(squares) / D + epsilon)
    key_clean = (clean_qkv[1].astype(f32) * inverse[2][:, None] * gain_k).astype(bf16)
    both = mixed(after(key_clean, *first), cross_values)
    cross_a = shift_spans(after(lanes(key_clean, 0, 2), cross_values), COLUMNS, crossers)
    cross_b = shift_spans(after(lanes(key_clean, 2, 3), cross_a), COLUMNS, crossers)
    last_a = [shift_columns(after(cross_a, *both), hop, "wrapped") for hop in steps]
    last_b = [shift_columns(after(cross_b, *last_a), hop, "wrapped") for hop in steps]

    hops = jnp.arange(1, CONTEXT + 1, dtype=jnp.int32)
    flags = jnp.concatenate([column >= hops, span >= hops, column + hops < COLUMNS]).astype(
        jnp.int32
    )
    gains = (gain_q[None, :], gain_k[None, :])
    fields = (clean_qkv, noise_qkv)

    def attend(head, heads, last, last_at, previous):
        out = attention_chunk(
            head, heads, flags, shares, inverse, gains, fields, attended_grad,
            (*first, *both), last, last_at, previous,
        )
        return out[:4], out[4:7], out[7]

    def send_back(blocks):
        return [shift_columns(block, -hop, "both") for hop, block in zip(steps, blocks)]

    def cross_back(received):
        total = jnp.zeros(received[0].shape, f32)
        for hop, block in zip(steps, received):
            total = total + jnp.where(column + hop >= COLUMNS, block, 0).astype(f32)
        return shift_spans(total.astype(bf16), -COLUMNS, crossers)

    results, back, inner_0 = attend(0, 2, last_a, 0, ())
    back_0 = send_back(back)
    crossed_0 = cross_back(back_0)
    results, kept, inner_1 = attend(2, 2, last_b, 0, results)
    results, back, inner_2 = attend(4, 1, last_b, 2, results)
    attended, *grads = results

    totals = head_sum(after(inner_0 + inner_1 + inner_2, *back_0)) / D
    high = lax.reduce_precision(totals[2:5], 8, 7)
    halves = jnp.stack([high, totals[2:5] - high]).reshape(2, CONTEXT, -1, 2 * HEAD_DIM)
    halves = jnp.pad(halves.astype(bf16), ((0, 0), (0, 0), (0, 14), (0, 0)))
    rows = attended_grad.shape[0]
    kept = [jnp.concatenate([block, halves[:, i]], axis=1) for i, block in enumerate(kept)]
    back_1 = send_back(after(tuple(kept), *back_0))
    crossed_1 = cross_back(back_1)
    back_2 = send_back(after(tuple(back), *back_1, crossed_0))
    crossed_2 = cross_back(after(tuple(back_2), crossed_1))

    def products_of(block):
        pieces = block[:, rows : rows + 2].astype(f32)
        return (pieces[0] + pieces[1]).reshape(-1)

    clean_inner = products_of(crossed_1)
    for hop, block in zip(steps, back_1):
        clean_inner = clean_inner + jnp.where(column + hop < COLUMNS, products_of(block), 0.0)
    cubes = jnp.stack(
        [
            inverse[0] ** 3 * totals[0],
            inverse[1] ** 3 * totals[1],
            inverse[2] ** 2 * clean_inner,
        ]
    )
    factors = jnp.concatenate([inverse[:3], cubes, cubes[:2]])
    clean_grads = None
    for head, heads, received, crossed in (
        (0, 2, back_0, crossed_0),
        (2, 2, back_1, crossed_1),
        (4, 1, back_2, crossed_2),
    ):
        clean_grads = finish_chunk(
            head, heads, flags, shares, factors, gains, fields, grads, received, crossed,
            clean_grads,
        )
    return (attended, clean_grads)


def solution(mesh):
    placed = (
        P(None, "tm", "head"),
        P(None, "tm", "head"),
        P("tm"),
        P("head"),
        P("head"),
        P("tm", "head"),
    )
    return jax.shard_map(
        on_device,
        mesh=mesh,
        in_specs=placed,
        out_specs=(P("tm", "head"), P(None, "tm", "head")),
        check_vma=False,
    )
```

```python
import math

import jax
import jax.numpy as jnp
from jax import lax
from jax.experimental import pallas as pl
from jax.experimental.pallas import tpu as pltpu
from jax.sharding import PartitionSpec as P

D = 5120
HEAD_DIM = 128
CONTEXT = 3
COLUMNS = 4
KEY_TILE = 512
VMEM_LIMIT = 60 * 2**20

epsilon = 1e-06
masked_score = -1e30
NT = (((1,), (1,)), ((), ()))
NN = (((1,), (0,)), ((), ()))


def dot(left, right, dims):
    return lax.dot_general(left, right, dims, preferred_element_type=jnp.float32)


def noise_share_of(timestep):
    level = timestep.astype(jnp.float32) / 1000.0
    return 5.0 * level / (1.0 + 4.0 * level)


def shift_spans(block, distance, columns=range(COLUMNS)):
    count = lax.axis_size("tm")
    route = [
        (i, i + distance)
        for i in range(count)
        if 0 <= i + distance < count and i % COLUMNS in columns
    ]
    return lax.ppermute(block, "tm", route)


def shift_columns(block, distance, kind):
    count = lax.axis_size("tm")
    route = []
    for i in range(count):
        row, column = divmod(i, COLUMNS)
        target = column + distance
        inside = 0 <= target < COLUMNS
        if kind == "both" or inside == (kind == "inside"):
            route.append((i, row * COLUMNS + target % COLUMNS))
    return lax.ppermute(block, "tm", route)


def as_columns(rows_ref):
    rows = rows_ref[...]
    return jnp.concatenate([rows] * (HEAD_DIM // 8), axis=0).T


def prepare_body(shares, clean, noise, sums, columns):
    f32 = jnp.float32
    keep, share = shares[0], shares[1]
    clean_key = clean[1].astype(f32)
    query = keep * clean[0].astype(f32) + share * noise[0].astype(f32)
    key = keep * clean_key + share * noise[1].astype(f32)
    lane = lax.broadcasted_iota(jnp.int32, columns.shape, 1)
    step = jnp.zeros(columns.shape, f32)
    for i, field in enumerate((query, key, clean_key)):
        step = jnp.where(lane == i, jnp.sum(field * field, axis=1, keepdims=True), step)

    @pl.when(pl.program_id(0) == 0)
    def _():
        columns[...] = step

    @pl.when(pl.program_id(0) > 0)
    def _():
        columns[...] += step

    @pl.when(pl.program_id(0) == pl.num_programs(0) - 1)
    def _():
        sums[...] = columns[...].T[0:8]


def prepare(shares, clean, noise):
    _, rows, width = clean.shape
    pair = pl.BlockSpec((2, rows, HEAD_DIM), lambda h: (0, 0, h))
    return pl.pallas_call(
        prepare_body,
        grid=(width // HEAD_DIM,),
        in_specs=[pl.BlockSpec(memory_space=pltpu.SMEM), pair, pair],
        out_specs=pl.BlockSpec((8, rows), lambda h: (0, 0)),
        out_shape=jax.ShapeDtypeStruct((8, rows), jnp.float32),
        scratch_shapes=[pltpu.VMEM((rows, HEAD_DIM), jnp.float32)],
        compiler_params=pltpu.CompilerParams(
            dimension_semantics=("arbitrary",), vmem_limit_bytes=VMEM_LIMIT
        ),
        cost_estimate=pl.CostEstimate(
            flops=rows * width * 12, bytes_accessed=rows * width * 8, transcendentals=0
        ),
    )(shares, clean, noise)


def attention_body(
    flags, shares, inverse, gain_q, gain_k, clean, noise, grad,
    first_1, first_2, first_3, both_1, both_2, both_3, last_1, last_2, last_3, *refs
):
    (attended, grad_query, grad_key, grad_value, back_1, back_2, back_3, inner,
     exps, probs, keys, values, cols, products) = refs[-14:]
    f32, bf16 = jnp.float32, jnp.bfloat16
    rows = grad.shape[0]
    scale = HEAD_DIM**-0.5
    exponent_scale = scale * math.log2(math.e)
    keep, share = shares[0], shares[1]
    gains_q, gains_k = gain_q[...], gain_k[...]
    sources = (
        (first_1, both_1, last_1),
        (first_2, both_2, last_2),
        (first_3, both_3, last_3),
    )
    backs = (back_1, back_2, back_3)

    @pl.when(pl.program_id(0) == 0)
    def _():
        products[...] = jnp.zeros_like(products)
        cols[...] = as_columns(inverse)

    field_query = keep * clean[0].astype(f32) + share * noise[0].astype(f32)
    field_key = keep * clean[1].astype(f32) + share * noise[1].astype(f32)
    field_value = keep * clean[2].astype(f32) + share * noise[2].astype(f32)
    queries = (field_query * cols[:, 0:1] * gains_q).astype(bf16)
    keys[0:rows] = (field_key * cols[:, 1:2] * gains_k).astype(bf16)
    values[0:rows] = field_value.astype(bf16)
    for hop, (first, both, last) in enumerate(sources):
        inside = flags[hop] > 0
        block = pl.ds((hop + 1) * rows, rows)
        keys[block] = jnp.where(inside, both[...], last[...])
        values[block] = jnp.where(inside, first[...], both[...])
    grads = grad[...]
    tiles = rows // KEY_TILE

    row_max = None
    for block in range(CONTEXT + 1):
        block_max = None
        for tile in range(tiles):
            part = pl.ds(block * rows + tile * KEY_TILE, KEY_TILE)
            scores = dot(keys[part], queries, NT)
            exps[part] = scores
            tile_max = jnp.max(scores, axis=0, keepdims=True)
            block_max = tile_max if block_max is None else jnp.maximum(block_max, tile_max)
        if block > 0:
            block_max = jnp.where(flags[2 + block] > 0, block_max, masked_score)
        row_max = block_max if row_max is None else jnp.maximum(row_max, block_max)
    offset = row_max * exponent_scale
    total = jnp.zeros((1, rows), f32)
    delta = jnp.zeros((1, rows), f32)
    for block in range(CONTEXT + 1):
        block_offset = offset
        if block > 0:
            block_offset = jnp.where(flags[2 + block] > 0, offset, -masked_score)
        for tile in range(tiles):
            part = pl.ds(block * rows + tile * KEY_TILE, KEY_TILE)
            exponent = jnp.exp2(exps[part] * exponent_scale - block_offset)
            grad_probs = dot(values[part], grads, NT)
            exps[part] = exponent
            probs[part] = grad_probs
            total = total + jnp.sum(exponent, axis=0, keepdims=True)
            delta = delta + jnp.sum(exponent * grad_probs, axis=0, keepdims=True)
    inverse_total = 1.0 / total
    delta = delta * inverse_total
    output = jnp.zeros((HEAD_DIM, rows), f32)
    query_grad = jnp.zeros((HEAD_DIM, rows), f32)
    lane = lax.broadcasted_iota(jnp.int32, (KEY_TILE, HEAD_DIM), 1)

    def add_product(here, index, product):
        product = jnp.sum(product, axis=1, keepdims=True)
        products[here] += jnp.where(lane == index, product, 0.0)

    for block in range(CONTEXT + 1):
        for tile in range(tiles):
            part = pl.ds(block * rows + tile * KEY_TILE, KEY_TILE)
            here = pl.ds(tile * KEY_TILE, KEY_TILE)
            attention = exps[part] * inverse_total
            weights = attention.astype(bf16)
            grad_scores = (attention * (probs[part] - delta) * scale).astype(bf16)
            output = output + dot(values[part].T, weights, NN)
            query_grad = query_grad + dot(keys[part].T, grad_scores, NN)
            value_part = dot(weights, grads, NN)
            key_part = dot(grad_scores, queries, NN)
            if block == 0:
                grad_key[here] = key_part
                grad_value[here] = value_part
                field = keep * clean[1, here].astype(f32) + share * noise[1, here].astype(f32)
                add_product(here, 1, field * gains_k * key_part)
            else:
                back = backs[block - 1]
                back[0, here] = key_part.astype(bf16)
                back[1, here] = value_part.astype(bf16)
                add_product(here, 1 + block, keys[part].astype(f32) * key_part)
    attended[...] = output.T.astype(bf16)
    grad_query[...] = query_grad.T
    for tile in range(tiles):
        here = pl.ds(tile * KEY_TILE, KEY_TILE)
        field = keep * clean[0, here].astype(f32) + share * noise[0, here].astype(f32)
        add_product(here, 0, field * gains_q * grad_query[here])

    @pl.when(pl.program_id(0) == pl.num_programs(0) - 1)
    def _():
        inner[...] = products[...].T[0:8]


def attention_chunk(first, heads, flags, shares, inverse, gains, fields, grad, gathered, last, last_at, spare, previous):
    rows, width = grad.shape
    here = lambda h: (0, first + h)
    f32, bf16 = jnp.float32, jnp.bfloat16
    smem = pl.BlockSpec(memory_space=pltpu.SMEM)
    small = pl.BlockSpec((8, rows), lambda h: (0, 0))
    wide = pl.BlockSpec((rows, HEAD_DIM), here)
    gain_spec = pl.BlockSpec((1, HEAD_DIM), here)
    field_spec = pl.BlockSpec((3, rows, HEAD_DIM), lambda h: (0, 0, first + h))
    last_spec = pl.BlockSpec((rows, HEAD_DIM), lambda h: (0, last_at + h))
    pair = pl.BlockSpec((2, rows, HEAD_DIM), lambda h: (0, 0, h))
    in_specs = (
        [smem, smem, small]
        + [gain_spec] * 2
        + [field_spec] * 2
        + [wide] * 7
        + [last_spec] * 3
    )
    operands = [flags, shares, inverse, *gains, *fields, grad, *gathered, *last]
    aliases = {}
    for position, array in enumerate(previous):
        aliases[len(operands)] = position
        operands.append(array)
        in_specs.append(pl.BlockSpec(memory_space=pl.ANY))
    back = jax.ShapeDtypeStruct((2, rows + spare, heads * HEAD_DIM), bf16)
    keys = (CONTEXT + 1) * rows
    flops = 6 * 2 * rows * keys * HEAD_DIM * heads
    return pl.pallas_call(
        attention_body,
        grid=(heads,),
        in_specs=in_specs,
        out_specs=[wide] * 4 + [pair] * 3 + [small],
        out_shape=[
            jax.ShapeDtypeStruct((rows, width), bf16),
            jax.ShapeDtypeStruct((rows, width), f32),
            jax.ShapeDtypeStruct((rows, width), f32),
            jax.ShapeDtypeStruct((rows, width), f32),
            back,
            back,
            back,
            jax.ShapeDtypeStruct((8, rows), f32),
        ],
        scratch_shapes=[
            pltpu.VMEM((keys, rows), f32),
            pltpu.VMEM((keys, rows), f32),
            pltpu.VMEM((keys, HEAD_DIM), bf16),
            pltpu.VMEM((keys, HEAD_DIM), bf16),
            pltpu.VMEM((rows, HEAD_DIM), f32),
            pltpu.VMEM((rows, HEAD_DIM), f32),
        ],
        input_output_aliases=aliases,
        compiler_params=pltpu.CompilerParams(
            dimension_semantics=("arbitrary",), vmem_limit_bytes=VMEM_LIMIT
        ),
        cost_estimate=pl.CostEstimate(
            flops=flops, bytes_accessed=heads * 4 * 2**20, transcendentals=rows * keys * heads
        ),
    )(*operands)


def finish_body(
    flags, shares, rows_ref, gain_q, gain_k, clean, noise, grad_query, grad_key, grad_value,
    in_1, in_2, in_3, crossed, *refs
):
    out, cols = refs[-2:]
    f32 = jnp.float32
    keep, share = shares[0], shares[1]

    @pl.when(pl.program_id(0) == 0)
    def _():
        cols[...] = as_columns(rows_ref)

    clean_key = clean[1].astype(f32)
    noisy_query = keep * clean[0].astype(f32) + share * noise[0].astype(f32)
    noisy_key = keep * clean_key + share * noise[1].astype(f32)
    key_grad = crossed[0].astype(f32)
    value_grad = crossed[1].astype(f32)
    for hop, received in enumerate((in_1, in_2, in_3)):
        inside = flags[6 + hop] > 0
        key_grad = key_grad + jnp.where(inside, received[0], 0).astype(f32)
        value_grad = value_grad + jnp.where(inside, received[1], 0).astype(f32)
    col = lambda i: cols[:, i : i + 1]
    gk = gain_k[...]
    out[0] = keep * (col(0) * gain_q[...] * grad_query[...] - noisy_query * col(3))
    own = col(1) * gk * grad_key[...] - noisy_key * col(4)
    out[1] = keep * own + (col(2) * gk * key_grad - clean_key * col(5))
    out[2] = keep * grad_value[...] + value_grad


def finish_chunk(first, heads, flags, shares, factors, gains, fields, grads, received, crossed, previous):
    _, rows, width = fields[0].shape
    here = lambda h: (0, first + h)
    wide = pl.BlockSpec((rows, HEAD_DIM), here)
    gain_spec = pl.BlockSpec((1, HEAD_DIM), here)
    two = pl.BlockSpec((2, rows, HEAD_DIM), lambda h: (0, 0, first + h))
    pair = pl.BlockSpec((2, rows, HEAD_DIM), lambda h: (0, 0, h))
    smem = pl.BlockSpec(memory_space=pltpu.SMEM)
    operands = [flags, shares, factors, *gains, *fields, *grads, *received, crossed]
    in_specs = (
        [smem, smem, pl.BlockSpec((8, rows), lambda h: (0, 0))]
        + [gain_spec] * 2
        + [two] * 2
        + [wide] * 3
        + [pair] * 4
    )
    aliases = {}
    if previous is not None:
        aliases[len(operands)] = 0
        operands.append(previous)
        in_specs.append(pl.BlockSpec(memory_space=pl.ANY))
    return pl.pallas_call(
        finish_body,
        grid=(heads,),
        in_specs=in_specs,
        out_specs=pl.BlockSpec((3, rows, HEAD_DIM), lambda h: (0, 0, first + h)),
        out_shape=jax.ShapeDtypeStruct((3, rows, width), jnp.float32),
        scratch_shapes=[pltpu.VMEM((rows, HEAD_DIM), jnp.float32)],
        input_output_aliases=aliases,
        compiler_params=pltpu.CompilerParams(
            dimension_semantics=("arbitrary",), vmem_limit_bytes=VMEM_LIMIT
        ),
        cost_estimate=pl.CostEstimate(
            flops=rows * HEAD_DIM * heads * 30,
            bytes_accessed=heads * rows * HEAD_DIM * 48,
            transcendentals=0,
        ),
    )(*operands)


def head_sum(block):
    count = lax.axis_size("head")
    distance = 1
    while distance < count:
        route = [(i, i ^ distance) for i in range(count)]
        block = block + lax.ppermute(block, "head", route)
        distance *= 2
    return block


def after(value, *earlier):
    return lax.optimization_barrier((value, *earlier))[0]


def on_device(clean_qkv, noise_qkv, timestep, gain_q, gain_k, attended_grad):
    f32, bf16 = jnp.float32, jnp.bfloat16
    span = lax.axis_index("tm")
    column = span % COLUMNS
    steps = range(1, CONTEXT + 1)
    crossers = range(1, COLUMNS)
    value_clean = clean_qkv[2]

    def lanes(block, first, heads):
        return block[:, first * HEAD_DIM : (first + heads) * HEAD_DIM]

    def mixed(own, wrap):
        return [
            shift_columns(jnp.where(column + hop < COLUMNS, own, wrap), hop, "both")
            for hop in steps
        ]

    cross_values = shift_spans(value_clean, COLUMNS, crossers)
    first = [shift_columns(value_clean, hop, "inside") for hop in steps]

    noise_share = noise_share_of(timestep[0])
    shares = jnp.stack([1.0 - noise_share, noise_share])
    squares = prepare(shares, clean_qkv, noise_qkv)
    inverse = lax.rsqrt(head_sum(squares) / D + epsilon)
    key_clean = (clean_qkv[1].astype(f32) * inverse[2][:, None] * gain_k).astype(bf16)
    both = mixed(after(key_clean, *first), cross_values)
    cross_a = shift_spans(after(lanes(key_clean, 0, 2), cross_values), COLUMNS, crossers)
    cross_b = shift_spans(after(lanes(key_clean, 2, 3), cross_a), COLUMNS, crossers)
    last_a = [shift_columns(after(cross_a, *both), hop, "wrapped") for hop in steps]
    last_b = [shift_columns(after(cross_b, *both), hop, "wrapped") for hop in steps]

    hops = jnp.arange(1, CONTEXT + 1, dtype=jnp.int32)
    flags = jnp.concatenate([column >= hops, span >= hops, column + hops < COLUMNS]).astype(
        jnp.int32
    )
    gains = (gain_q[None, :], gain_k[None, :])
    fields = (clean_qkv, noise_qkv)

    def attend(head, heads, last, last_at, spare, previous):
        out = attention_chunk(
            head, heads, flags, shares, inverse, gains, fields, attended_grad,
            (*first, *both), last, last_at, spare, previous,
        )
        return out[:4], out[4:7], out[7]

    def send_back(blocks):
        return [shift_columns(block, -hop, "both") for hop, block in zip(steps, blocks)]

    def cross_back(received):
        total = jnp.zeros(received[0].shape, f32)
        for hop, block in zip(steps, received):
            total = total + jnp.where(column + hop >= COLUMNS, block, 0).astype(f32)
        return shift_spans(total.astype(bf16), -COLUMNS, crossers)

    results, back, inner_0 = attend(0, 2, last_a, 0, 0, ())
    back_0 = send_back(back)
    crossed_0 = cross_back(back_0)
    results, kept, inner_1 = attend(2, 2, last_b, 0, 16, results)
    results, back, inner_2 = attend(4, 1, last_b, 2, 0, results)
    attended, *grads = results

    totals = head_sum(after(inner_0 + inner_1 + inner_2, *back_0)) / D
    high = lax.reduce_precision(totals[2:5], 8, 7)
    halves = jnp.stack([high, totals[2:5] - high]).reshape(2, CONTEXT, -1, 2 * HEAD_DIM)
    halves = jnp.pad(halves.astype(bf16), ((0, 0), (0, 0), (0, 14), (0, 0)))
    rows = attended_grad.shape[0]
    kept = [
        lax.dynamic_update_slice(block, halves[:, i], (0, rows, 0))
        for i, block in enumerate(kept)
    ]
    back_1 = send_back(after(tuple(kept), *back_0))
    crossed_1 = cross_back(back_1)
    back_2 = send_back(after(tuple(back), *back_1, crossed_0))
    crossed_2 = cross_back(back_2)

    def products_of(block):
        pieces = block[:, rows : rows + 2].astype(f32)
        return (pieces[0] + pieces[1]).reshape(-1)

    clean_inner = products_of(crossed_1)
    for hop, block in zip(steps, back_1):
        clean_inner = clean_inner + jnp.where(column + hop < COLUMNS, products_of(block), 0.0)
    cubes = jnp.stack(
        [
            inverse[0] ** 3 * totals[0],
            inverse[1] ** 3 * totals[1],
            inverse[2] ** 2 * clean_inner,
        ]
    )
    factors = jnp.concatenate([inverse[:3], cubes, cubes[:2]])
    clean_grads = None
    for head, heads, received, crossed in (
        (0, 2, back_0, crossed_0),
        (2, 2, back_1, crossed_1),
        (4, 1, back_2, crossed_2),
    ):
        clean_grads = finish_chunk(
            head, heads, flags, shares, factors, gains, fields, grads, received, crossed,
            clean_grads,
        )
    return (attended, clean_grads)


def solution(mesh):
    placed = (
        P(None, "tm", "head"),
        P(None, "tm", "head"),
        P("tm"),
        P("head"),
        P("head"),
        P("tm", "head"),
    )
    return jax.shard_map(
        on_device,
        mesh=mesh,
        in_specs=placed,
        out_specs=(P("tm", "head"), P(None, "tm", "head")),
        check_vma=False,
    )
```

```python
import math

import jax
import jax.numpy as jnp
from jax import lax
from jax.experimental import pallas as pl
from jax.experimental.pallas import tpu as pltpu
from jax.sharding import PartitionSpec as P

D = 5120
HEAD_DIM = 128
CONTEXT = 3
COLUMNS = 4
KEY_TILE = 512
VMEM_LIMIT = 60 * 2**20

epsilon = 1e-06
masked_score = -1e30
NT = (((1,), (1,)), ((), ()))
NN = (((1,), (0,)), ((), ()))


def dot(left, right, dims):
    return lax.dot_general(left, right, dims, preferred_element_type=jnp.float32)


def noise_share_of(timestep):
    level = timestep.astype(jnp.float32) / 1000.0
    return 5.0 * level / (1.0 + 4.0 * level)


def shift_spans(block, distance, columns=range(COLUMNS)):
    count = lax.axis_size("tm")
    route = [
        (i, i + distance)
        for i in range(count)
        if 0 <= i + distance < count and i % COLUMNS in columns
    ]
    return lax.ppermute(block, "tm", route)


def shift_columns(block, distance, kind):
    count = lax.axis_size("tm")
    route = []
    for i in range(count):
        row, column = divmod(i, COLUMNS)
        target = column + distance
        inside = 0 <= target < COLUMNS
        if kind == "both" or inside == (kind == "inside"):
            route.append((i, row * COLUMNS + target % COLUMNS))
    return lax.ppermute(block, "tm", route)


def as_columns(rows_ref):
    rows = rows_ref[...]
    return jnp.concatenate([rows] * (HEAD_DIM // 8), axis=0).T


def prepare_body(shares, clean, noise, sums, columns):
    f32 = jnp.float32
    keep, share = shares[0], shares[1]
    clean_key = clean[1].astype(f32)
    query = keep * clean[0].astype(f32) + share * noise[0].astype(f32)
    key = keep * clean_key + share * noise[1].astype(f32)
    lane = lax.broadcasted_iota(jnp.int32, columns.shape, 1)
    step = jnp.zeros(columns.shape, f32)
    for i, field in enumerate((query, key, clean_key)):
        step = jnp.where(lane == i, jnp.sum(field * field, axis=1, keepdims=True), step)

    @pl.when(pl.program_id(0) == 0)
    def _():
        columns[...] = step

    @pl.when(pl.program_id(0) > 0)
    def _():
        columns[...] += step

    @pl.when(pl.program_id(0) == pl.num_programs(0) - 1)
    def _():
        sums[...] = columns[...].T[0:8]


def prepare(shares, clean, noise):
    _, rows, width = clean.shape
    pair = pl.BlockSpec((2, rows, HEAD_DIM), lambda h: (0, 0, h))
    return pl.pallas_call(
        prepare_body,
        grid=(width // HEAD_DIM,),
        in_specs=[pl.BlockSpec(memory_space=pltpu.SMEM), pair, pair],
        out_specs=pl.BlockSpec((8, rows), lambda h: (0, 0)),
        out_shape=jax.ShapeDtypeStruct((8, rows), jnp.float32),
        scratch_shapes=[pltpu.VMEM((rows, HEAD_DIM), jnp.float32)],
        compiler_params=pltpu.CompilerParams(
            dimension_semantics=("arbitrary",), vmem_limit_bytes=VMEM_LIMIT
        ),
        cost_estimate=pl.CostEstimate(
            flops=rows * width * 12, bytes_accessed=rows * width * 8, transcendentals=0
        ),
    )(shares, clean, noise)


def attention_body(
    flags, shares, inverse, gain_q, gain_k, clean, noise, grad,
    first_1, first_2, first_3, both_1, both_2, both_3, last_1, last_2, last_3, *refs
):
    (attended, grad_query, grad_key, grad_value, back_1, back_2, back_3, inner,
     exps, probs, keys, values, cols, products) = refs[-14:]
    f32, bf16 = jnp.float32, jnp.bfloat16
    rows = grad.shape[0]
    scale = HEAD_DIM**-0.5
    exponent_scale = scale * math.log2(math.e)
    keep, share = shares[0], shares[1]
    gains_q, gains_k = gain_q[...], gain_k[...]
    sources = (
        (first_1, both_1, last_1),
        (first_2, both_2, last_2),
        (first_3, both_3, last_3),
    )
    backs = (back_1, back_2, back_3)

    @pl.when(pl.program_id(0) == 0)
    def _():
        products[...] = jnp.zeros_like(products)
        cols[...] = as_columns(inverse)

    field_query = keep * clean[0].astype(f32) + share * noise[0].astype(f32)
    field_key = keep * clean[1].astype(f32) + share * noise[1].astype(f32)
    field_value = keep * clean[2].astype(f32) + share * noise[2].astype(f32)
    queries = (field_query * cols[:, 0:1] * gains_q).astype(bf16)
    keys[0:rows] = (field_key * cols[:, 1:2] * gains_k).astype(bf16)
    values[0:rows] = field_value.astype(bf16)
    for hop, (first, both, last) in enumerate(sources):
        inside = flags[hop] > 0
        block = pl.ds((hop + 1) * rows, rows)
        keys[block] = jnp.where(inside, both[...], last[...])
        values[block] = jnp.where(inside, first[...], both[...])
    grads = grad[...]
    tiles = rows // KEY_TILE

    row_max = None
    for block in range(CONTEXT + 1):
        block_max = None
        for tile in range(tiles):
            part = pl.ds(block * rows + tile * KEY_TILE, KEY_TILE)
            scores = dot(keys[part], queries, NT)
            exps[part] = scores
            tile_max = jnp.max(scores, axis=0, keepdims=True)
            block_max = tile_max if block_max is None else jnp.maximum(block_max, tile_max)
        if block > 0:
            block_max = jnp.where(flags[2 + block] > 0, block_max, masked_score)
        row_max = block_max if row_max is None else jnp.maximum(row_max, block_max)
    offset = row_max * exponent_scale
    total = jnp.zeros((1, rows), f32)
    delta = jnp.zeros((1, rows), f32)
    for block in range(CONTEXT + 1):
        block_offset = offset
        if block > 0:
            block_offset = jnp.where(flags[2 + block] > 0, offset, -masked_score)
        for tile in range(tiles):
            part = pl.ds(block * rows + tile * KEY_TILE, KEY_TILE)
            exponent = jnp.exp2(exps[part] * exponent_scale - block_offset)
            grad_probs = dot(values[part], grads, NT)
            exps[part] = exponent
            probs[part] = grad_probs
            total = total + jnp.sum(exponent, axis=0, keepdims=True)
            delta = delta + jnp.sum(exponent * grad_probs, axis=0, keepdims=True)
    inverse_total = 1.0 / total
    delta = delta * inverse_total
    output = jnp.zeros((HEAD_DIM, rows), f32)
    query_grad = jnp.zeros((HEAD_DIM, rows), f32)
    lane = lax.broadcasted_iota(jnp.int32, (KEY_TILE, HEAD_DIM), 1)

    def add_product(here, index, product):
        product = jnp.sum(product, axis=1, keepdims=True)
        products[here] += jnp.where(lane == index, product, 0.0)

    for block in range(CONTEXT + 1):
        for tile in range(tiles):
            part = pl.ds(block * rows + tile * KEY_TILE, KEY_TILE)
            here = pl.ds(tile * KEY_TILE, KEY_TILE)
            attention = exps[part] * inverse_total
            weights = attention.astype(bf16)
            grad_scores = (attention * (probs[part] - delta) * scale).astype(bf16)
            output = output + dot(values[part].T, weights, NN)
            query_grad = query_grad + dot(keys[part].T, grad_scores, NN)
            value_part = dot(weights, grads, NN)
            key_part = dot(grad_scores, queries, NN)
            if block == 0:
                grad_key[here] = key_part
                grad_value[here] = value_part
                field = keep * clean[1, here].astype(f32) + share * noise[1, here].astype(f32)
                add_product(here, 1, field * gains_k * key_part)
            else:
                back = backs[block - 1]
                back[0, here] = key_part.astype(bf16)
                back[1, here] = value_part.astype(bf16)
                add_product(here, 1 + block, keys[part].astype(f32) * key_part)
    attended[...] = output.T.astype(bf16)
    grad_query[...] = query_grad.T
    for tile in range(tiles):
        here = pl.ds(tile * KEY_TILE, KEY_TILE)
        field = keep * clean[0, here].astype(f32) + share * noise[0, here].astype(f32)
        add_product(here, 0, field * gains_q * grad_query[here])

    @pl.when(pl.program_id(0) == pl.num_programs(0) - 1)
    def _():
        inner[...] = products[...].T[0:8]


def attention_chunk(first, heads, flags, shares, inverse, gains, fields, grad, gathered, last, last_at, spare, previous):
    rows, width = grad.shape
    here = lambda h: (0, first + h)
    f32, bf16 = jnp.float32, jnp.bfloat16
    smem = pl.BlockSpec(memory_space=pltpu.SMEM)
    small = pl.BlockSpec((8, rows), lambda h: (0, 0))
    wide = pl.BlockSpec((rows, HEAD_DIM), here)
    gain_spec = pl.BlockSpec((1, HEAD_DIM), here)
    field_spec = pl.BlockSpec((3, rows, HEAD_DIM), lambda h: (0, 0, first + h))
    last_spec = pl.BlockSpec((rows, HEAD_DIM), lambda h: (0, last_at + h))
    pair = pl.BlockSpec((2, rows, HEAD_DIM), lambda h: (0, 0, h))
    in_specs = (
        [smem, smem, small]
        + [gain_spec] * 2
        + [field_spec] * 2
        + [wide] * 7
        + [last_spec] * 3
    )
    operands = [flags, shares, inverse, *gains, *fields, grad, *gathered, *last]
    aliases = {}
    for position, array in enumerate(previous):
        aliases[len(operands)] = position
        operands.append(array)
        in_specs.append(pl.BlockSpec(memory_space=pl.ANY))
    back = jax.ShapeDtypeStruct((2, rows + spare, heads * HEAD_DIM), bf16)
    keys = (CONTEXT + 1) * rows
    flops = 6 * 2 * rows * keys * HEAD_DIM * heads
    return pl.pallas_call(
        attention_body,
        grid=(heads,),
        in_specs=in_specs,
        out_specs=[wide] * 4 + [pair] * 3 + [small],
        out_shape=[
            jax.ShapeDtypeStruct((rows, width), bf16),
            jax.ShapeDtypeStruct((rows, width), f32),
            jax.ShapeDtypeStruct((rows, width), f32),
            jax.ShapeDtypeStruct((rows, width), f32),
            back,
            back,
            back,
            jax.ShapeDtypeStruct((8, rows), f32),
        ],
        scratch_shapes=[
            pltpu.VMEM((keys, rows), f32),
            pltpu.VMEM((keys, rows), f32),
            pltpu.VMEM((keys, HEAD_DIM), bf16),
            pltpu.VMEM((keys, HEAD_DIM), bf16),
            pltpu.VMEM((rows, HEAD_DIM), f32),
            pltpu.VMEM((rows, HEAD_DIM), f32),
        ],
        input_output_aliases=aliases,
        compiler_params=pltpu.CompilerParams(
            dimension_semantics=("arbitrary",), vmem_limit_bytes=VMEM_LIMIT
        ),
        cost_estimate=pl.CostEstimate(
            flops=flops, bytes_accessed=heads * 4 * 2**20, transcendentals=rows * keys * heads
        ),
    )(*operands)


def finish_body(
    flags, shares, rows_ref, gain_q, gain_k, clean, noise, grad_query, grad_key, grad_value,
    in_1, in_2, in_3, crossed, *refs
):
    out, cols = refs[-2:]
    f32 = jnp.float32
    keep, share = shares[0], shares[1]

    @pl.when(pl.program_id(0) == 0)
    def _():
        cols[...] = as_columns(rows_ref)

    clean_key = clean[1].astype(f32)
    noisy_query = keep * clean[0].astype(f32) + share * noise[0].astype(f32)
    noisy_key = keep * clean_key + share * noise[1].astype(f32)
    key_grad = crossed[0].astype(f32)
    value_grad = crossed[1].astype(f32)
    for hop, received in enumerate((in_1, in_2, in_3)):
        inside = flags[6 + hop] > 0
        key_grad = key_grad + jnp.where(inside, received[0], 0).astype(f32)
        value_grad = value_grad + jnp.where(inside, received[1], 0).astype(f32)
    col = lambda i: cols[:, i : i + 1]
    gk = gain_k[...]
    out[0] = keep * (col(0) * gain_q[...] * grad_query[...] - noisy_query * col(3))
    own = col(1) * gk * grad_key[...] - noisy_key * col(4)
    out[1] = keep * own + (col(2) * gk * key_grad - clean_key * col(5))
    out[2] = keep * grad_value[...] + value_grad


def finish_chunk(first, heads, flags, shares, factors, gains, fields, grads, received, crossed, previous):
    _, rows, width = fields[0].shape
    here = lambda h: (0, first + h)
    wide = pl.BlockSpec((rows, HEAD_DIM), here)
    gain_spec = pl.BlockSpec((1, HEAD_DIM), here)
    two = pl.BlockSpec((2, rows, HEAD_DIM), lambda h: (0, 0, first + h))
    pair = pl.BlockSpec((2, rows, HEAD_DIM), lambda h: (0, 0, h))
    smem = pl.BlockSpec(memory_space=pltpu.SMEM)
    operands = [flags, shares, factors, *gains, *fields, *grads, *received, crossed]
    in_specs = (
        [smem, smem, pl.BlockSpec((8, rows), lambda h: (0, 0))]
        + [gain_spec] * 2
        + [two] * 2
        + [wide] * 3
        + [pair] * 4
    )
    aliases = {}
    if previous is not None:
        aliases[len(operands)] = 0
        operands.append(previous)
        in_specs.append(pl.BlockSpec(memory_space=pl.ANY))
    return pl.pallas_call(
        finish_body,
        grid=(heads,),
        in_specs=in_specs,
        out_specs=pl.BlockSpec((3, rows, HEAD_DIM), lambda h: (0, 0, first + h)),
        out_shape=jax.ShapeDtypeStruct((3, rows, width), jnp.float32),
        scratch_shapes=[pltpu.VMEM((rows, HEAD_DIM), jnp.float32)],
        input_output_aliases=aliases,
        compiler_params=pltpu.CompilerParams(
            dimension_semantics=("arbitrary",), vmem_limit_bytes=VMEM_LIMIT
        ),
        cost_estimate=pl.CostEstimate(
            flops=rows * HEAD_DIM * heads * 30,
            bytes_accessed=heads * rows * HEAD_DIM * 48,
            transcendentals=0,
        ),
    )(*operands)


def head_sum(block):
    count = lax.axis_size("head")
    distance = 1
    while distance < count:
        route = [(i, i ^ distance) for i in range(count)]
        block = block + lax.ppermute(block, "head", route)
        distance *= 2
    return block


def after(value, *earlier):
    return lax.optimization_barrier((value, *earlier))[0]


def on_device(clean_qkv, noise_qkv, timestep, gain_q, gain_k, attended_grad):
    f32, bf16 = jnp.float32, jnp.bfloat16
    span = lax.axis_index("tm")
    column = span % COLUMNS
    steps = range(1, CONTEXT + 1)
    crossers = range(1, COLUMNS)
    value_clean = clean_qkv[2]

    def lanes(block, first, heads):
        return block[:, first * HEAD_DIM : (first + heads) * HEAD_DIM]

    def mixed(own, wrap):
        return [
            shift_columns(jnp.where(column + hop < COLUMNS, own, wrap), hop, "both")
            for hop in steps
        ]

    cross_values = shift_spans(value_clean, COLUMNS, crossers)
    first = [shift_columns(value_clean, hop, "inside") for hop in steps]

    noise_share = noise_share_of(timestep[0])
    shares = jnp.stack([1.0 - noise_share, noise_share])
    squares = prepare(shares, clean_qkv, noise_qkv)
    inverse = lax.rsqrt(head_sum(squares) / D + epsilon)
    key_clean = (clean_qkv[1].astype(f32) * inverse[2][:, None] * gain_k).astype(bf16)
    both = mixed(after(key_clean, *first), cross_values)
    cross_a = shift_spans(after(lanes(key_clean, 0, 2), cross_values), COLUMNS, crossers)
    cross_b = shift_spans(after(lanes(key_clean, 2, 3), cross_a), COLUMNS, crossers)
    last_a = [shift_columns(cross_a, hop, "wrapped") for hop in steps]
    last_b = [shift_columns(after(cross_b, *both), hop, "wrapped") for hop in steps]

    hops = jnp.arange(1, CONTEXT + 1, dtype=jnp.int32)
    flags = jnp.concatenate([column >= hops, span >= hops, column + hops < COLUMNS]).astype(
        jnp.int32
    )
    gains = (gain_q[None, :], gain_k[None, :])
    fields = (clean_qkv, noise_qkv)

    def attend(head, heads, last, last_at, spare, previous):
        out = attention_chunk(
            head, heads, flags, shares, inverse, gains, fields, attended_grad,
            (*first, *both), last, last_at, spare, previous,
        )
        return out[:4], out[4:7], out[7]

    def send_back(blocks):
        return [shift_columns(block, -hop, "both") for hop, block in zip(steps, blocks)]

    def cross_back(received):
        total = jnp.zeros(received[0].shape, f32)
        for hop, block in zip(steps, received):
            total = total + jnp.where(column + hop >= COLUMNS, block, 0).astype(f32)
        return shift_spans(total.astype(bf16), -COLUMNS, crossers)

    results, back, inner_0 = attend(0, 2, last_a, 0, 0, ())
    back_0 = send_back(back)
    crossed_0 = cross_back(back_0)
    results, kept, inner_1 = attend(2, 2, last_b, 0, 16, results)
    results, back, inner_2 = attend(4, 1, last_b, 2, 0, results)
    attended, *grads = results

    totals = head_sum(after(inner_0 + inner_1 + inner_2, *back_0)) / D
    high = lax.reduce_precision(totals[2:5], 8, 7)
    halves = jnp.stack([high, totals[2:5] - high]).reshape(2, CONTEXT, -1, 2 * HEAD_DIM)
    halves = jnp.pad(halves.astype(bf16), ((0, 0), (0, 0), (0, 14), (0, 0)))
    rows = attended_grad.shape[0]
    kept = [
        lax.dynamic_update_slice(block, halves[:, i], (0, rows, 0))
        for i, block in enumerate(kept)
    ]
    back_1 = send_back(after(tuple(kept), *back_0))
    crossed_1 = cross_back(back_1)
    back_2 = send_back(after(tuple(back), *back_1, crossed_0))
    crossed_2 = cross_back(back_2)

    def products_of(block):
        pieces = block[:, rows : rows + 2].astype(f32)
        return (pieces[0] + pieces[1]).reshape(-1)

    clean_inner = products_of(crossed_1)
    for hop, block in zip(steps, back_1):
        clean_inner = clean_inner + jnp.where(column + hop < COLUMNS, products_of(block), 0.0)
    cubes = jnp.stack(
        [
            inverse[0] ** 3 * totals[0],
            inverse[1] ** 3 * totals[1],
            inverse[2] ** 2 * clean_inner,
        ]
    )
    factors = jnp.concatenate([inverse[:3], cubes, cubes[:2]])
    clean_grads = None
    for head, heads, received, crossed in (
        (0, 2, back_0, crossed_0),
        (2, 2, back_1, crossed_1),
        (4, 1, back_2, crossed_2),
    ):
        clean_grads = finish_chunk(
            head, heads, flags, shares, factors, gains, fields, grads, received, crossed,
            clean_grads,
        )
    return (attended, clean_grads)


def solution(mesh):
    placed = (
        P(None, "tm", "head"),
        P(None, "tm", "head"),
        P("tm"),
        P("head"),
        P("head"),
        P("tm", "head"),
    )
    return jax.shard_map(
        on_device,
        mesh=mesh,
        in_specs=placed,
        out_specs=(P("tm", "head"), P(None, "tm", "head")),
        check_vma=False,
    )
```

```python
import math

import jax
import jax.numpy as jnp
from jax import lax
from jax.experimental import pallas as pl
from jax.experimental.pallas import tpu as pltpu
from jax.sharding import PartitionSpec as P

D = 5120
HEAD_DIM = 128
CONTEXT = 3
COLUMNS = 4
KEY_TILE = 512
VMEM_LIMIT = 60 * 2**20

epsilon = 1e-06
masked_score = -1e30
NT = (((1,), (1,)), ((), ()))
NN = (((1,), (0,)), ((), ()))


def dot(left, right, dims):
    return lax.dot_general(left, right, dims, preferred_element_type=jnp.float32)


def noise_share_of(timestep):
    level = timestep.astype(jnp.float32) / 1000.0
    return 5.0 * level / (1.0 + 4.0 * level)


def shift_spans(block, distance, columns=range(COLUMNS)):
    count = lax.axis_size("tm")
    route = [
        (i, i + distance)
        for i in range(count)
        if 0 <= i + distance < count and i % COLUMNS in columns
    ]
    return lax.ppermute(block, "tm", route)


def shift_columns(block, distance, kind):
    count = lax.axis_size("tm")
    route = []
    for i in range(count):
        row, column = divmod(i, COLUMNS)
        target = column + distance
        inside = 0 <= target < COLUMNS
        if kind == "both" or inside == (kind == "inside"):
            route.append((i, row * COLUMNS + target % COLUMNS))
    return lax.ppermute(block, "tm", route)


def as_columns(rows_ref):
    rows = rows_ref[...]
    return jnp.concatenate([rows] * (HEAD_DIM // 8), axis=0).T


def prepare_body(shares, clean, noise, sums, columns):
    f32 = jnp.float32
    keep, share = shares[0], shares[1]
    clean_key = clean[1].astype(f32)
    query = keep * clean[0].astype(f32) + share * noise[0].astype(f32)
    key = keep * clean_key + share * noise[1].astype(f32)
    lane = lax.broadcasted_iota(jnp.int32, columns.shape, 1)
    step = jnp.zeros(columns.shape, f32)
    for i, field in enumerate((query, key, clean_key)):
        step = jnp.where(lane == i, jnp.sum(field * field, axis=1, keepdims=True), step)

    @pl.when(pl.program_id(0) == 0)
    def _():
        columns[...] = step

    @pl.when(pl.program_id(0) > 0)
    def _():
        columns[...] += step

    @pl.when(pl.program_id(0) == pl.num_programs(0) - 1)
    def _():
        sums[...] = columns[...].T[0:8]


def prepare(shares, clean, noise):
    _, rows, width = clean.shape
    pair = pl.BlockSpec((2, rows, HEAD_DIM), lambda h: (0, 0, h))
    return pl.pallas_call(
        prepare_body,
        grid=(width // HEAD_DIM,),
        in_specs=[pl.BlockSpec(memory_space=pltpu.SMEM), pair, pair],
        out_specs=pl.BlockSpec((8, rows), lambda h: (0, 0)),
        out_shape=jax.ShapeDtypeStruct((8, rows), jnp.float32),
        scratch_shapes=[pltpu.VMEM((rows, HEAD_DIM), jnp.float32)],
        compiler_params=pltpu.CompilerParams(
            dimension_semantics=("arbitrary",), vmem_limit_bytes=VMEM_LIMIT
        ),
        cost_estimate=pl.CostEstimate(
            flops=rows * width * 12, bytes_accessed=rows * width * 8, transcendentals=0
        ),
    )(shares, clean, noise)


def attention_body(
    flags, shares, inverse, gain_q, gain_k, clean, noise, grad,
    first_1, first_2, first_3, both_1, both_2, both_3, last_1, last_2, last_3, *refs
):
    (attended, grad_query, grad_key, grad_value, back_1, back_2, back_3, inner,
     exps, probs, keys, values, cols, products) = refs[-14:]
    f32, bf16 = jnp.float32, jnp.bfloat16
    rows = grad.shape[0]
    scale = HEAD_DIM**-0.5
    exponent_scale = scale * math.log2(math.e)
    keep, share = shares[0], shares[1]
    gains_q, gains_k = gain_q[...], gain_k[...]
    sources = (
        (first_1, both_1, last_1),
        (first_2, both_2, last_2),
        (first_3, both_3, last_3),
    )
    backs = (back_1, back_2, back_3)

    @pl.when(pl.program_id(0) == 0)
    def _():
        products[...] = jnp.zeros_like(products)
        cols[...] = as_columns(inverse)

    field_query = keep * clean[0].astype(f32) + share * noise[0].astype(f32)
    field_key = keep * clean[1].astype(f32) + share * noise[1].astype(f32)
    field_value = keep * clean[2].astype(f32) + share * noise[2].astype(f32)
    queries = (field_query * cols[:, 0:1] * gains_q).astype(bf16)
    keys[0:rows] = (field_key * cols[:, 1:2] * gains_k).astype(bf16)
    values[0:rows] = field_value.astype(bf16)
    for hop, (first, both, last) in enumerate(sources):
        inside = flags[hop] > 0
        block = pl.ds((hop + 1) * rows, rows)
        keys[block] = jnp.where(inside, both[...], last[...])
        values[block] = jnp.where(inside, first[...], both[...])
    grads = grad[...]
    tiles = rows // KEY_TILE

    row_max = None
    for block in range(CONTEXT + 1):
        block_max = None
        for tile in range(tiles):
            part = pl.ds(block * rows + tile * KEY_TILE, KEY_TILE)
            scores = dot(keys[part], queries, NT)
            exps[part] = scores
            tile_max = jnp.max(scores, axis=0, keepdims=True)
            block_max = tile_max if block_max is None else jnp.maximum(block_max, tile_max)
        if block > 0:
            block_max = jnp.where(flags[2 + block] > 0, block_max, masked_score)
        row_max = block_max if row_max is None else jnp.maximum(row_max, block_max)
    offset = row_max * exponent_scale
    total = jnp.zeros((1, rows), f32)
    delta = jnp.zeros((1, rows), f32)
    for block in range(CONTEXT + 1):
        block_offset = offset
        if block > 0:
            block_offset = jnp.where(flags[2 + block] > 0, offset, -masked_score)
        for tile in range(tiles):
            part = pl.ds(block * rows + tile * KEY_TILE, KEY_TILE)
            exponent = jnp.exp2(exps[part] * exponent_scale - block_offset)
            grad_probs = dot(values[part], grads, NT)
            exps[part] = exponent
            probs[part] = grad_probs
            total = total + jnp.sum(exponent, axis=0, keepdims=True)
            delta = delta + jnp.sum(exponent * grad_probs, axis=0, keepdims=True)
    inverse_total = 1.0 / total
    delta = delta * inverse_total
    output = jnp.zeros((HEAD_DIM, rows), f32)
    query_grad = jnp.zeros((HEAD_DIM, rows), f32)
    lane = lax.broadcasted_iota(jnp.int32, (KEY_TILE, HEAD_DIM), 1)

    def add_product(here, index, product):
        product = jnp.sum(product, axis=1, keepdims=True)
        products[here] += jnp.where(lane == index, product, 0.0)

    for block in range(CONTEXT + 1):
        for tile in range(tiles):
            part = pl.ds(block * rows + tile * KEY_TILE, KEY_TILE)
            here = pl.ds(tile * KEY_TILE, KEY_TILE)
            attention = exps[part] * inverse_total
            weights = attention.astype(bf16)
            grad_scores = (attention * (probs[part] - delta) * scale).astype(bf16)
            output = output + dot(values[part].T, weights, NN)
            query_grad = query_grad + dot(keys[part].T, grad_scores, NN)
            value_part = dot(weights, grads, NN)
            key_part = dot(grad_scores, queries, NN)
            if block == 0:
                grad_key[here] = key_part
                grad_value[here] = value_part
                field = keep * clean[1, here].astype(f32) + share * noise[1, here].astype(f32)
                add_product(here, 1, field * gains_k * key_part)
            else:
                back = backs[block - 1]
                back[0, here] = key_part.astype(bf16)
                back[1, here] = value_part.astype(bf16)
                add_product(here, 1 + block, keys[part].astype(f32) * key_part)
    attended[...] = output.T.astype(bf16)
    grad_query[...] = query_grad.T
    for tile in range(tiles):
        here = pl.ds(tile * KEY_TILE, KEY_TILE)
        field = keep * clean[0, here].astype(f32) + share * noise[0, here].astype(f32)
        add_product(here, 0, field * gains_q * grad_query[here])

    @pl.when(pl.program_id(0) == pl.num_programs(0) - 1)
    def _():
        inner[...] = products[...].T[0:8]


def attention_chunk(first, heads, flags, shares, inverse, gains, fields, grad, gathered, last, last_at, spare, previous):
    rows, width = grad.shape
    here = lambda h: (0, first + h)
    f32, bf16 = jnp.float32, jnp.bfloat16
    smem = pl.BlockSpec(memory_space=pltpu.SMEM)
    small = pl.BlockSpec((8, rows), lambda h: (0, 0))
    wide = pl.BlockSpec((rows, HEAD_DIM), here)
    gain_spec = pl.BlockSpec((1, HEAD_DIM), here)
    field_spec = pl.BlockSpec((3, rows, HEAD_DIM), lambda h: (0, 0, first + h))
    last_spec = pl.BlockSpec((rows, HEAD_DIM), lambda h: (0, last_at + h))
    pair = pl.BlockSpec((2, rows, HEAD_DIM), lambda h: (0, 0, h))
    in_specs = (
        [smem, smem, small]
        + [gain_spec] * 2
        + [field_spec] * 2
        + [wide] * 7
        + [last_spec] * 3
    )
    operands = [flags, shares, inverse, *gains, *fields, grad, *gathered, *last]
    aliases = {}
    for position, array in enumerate(previous):
        aliases[len(operands)] = position
        operands.append(array)
        in_specs.append(pl.BlockSpec(memory_space=pl.ANY))
    back = jax.ShapeDtypeStruct((2, rows + spare, heads * HEAD_DIM), bf16)
    keys = (CONTEXT + 1) * rows
    flops = 6 * 2 * rows * keys * HEAD_DIM * heads
    return pl.pallas_call(
        attention_body,
        grid=(heads,),
        in_specs=in_specs,
        out_specs=[wide] * 4 + [pair] * 3 + [small],
        out_shape=[
            jax.ShapeDtypeStruct((rows, width), bf16),
            jax.ShapeDtypeStruct((rows, width), f32),
            jax.ShapeDtypeStruct((rows, width), f32),
            jax.ShapeDtypeStruct((rows, width), f32),
            back,
            back,
            back,
            jax.ShapeDtypeStruct((8, rows), f32),
        ],
        scratch_shapes=[
            pltpu.VMEM((keys, rows), f32),
            pltpu.VMEM((keys, rows), f32),
            pltpu.VMEM((keys, HEAD_DIM), bf16),
            pltpu.VMEM((keys, HEAD_DIM), bf16),
            pltpu.VMEM((rows, HEAD_DIM), f32),
            pltpu.VMEM((rows, HEAD_DIM), f32),
        ],
        input_output_aliases=aliases,
        compiler_params=pltpu.CompilerParams(
            dimension_semantics=("arbitrary",), vmem_limit_bytes=VMEM_LIMIT
        ),
        cost_estimate=pl.CostEstimate(
            flops=flops, bytes_accessed=heads * 4 * 2**20, transcendentals=rows * keys * heads
        ),
    )(*operands)


def finish_body(
    flags, shares, rows_ref, gain_q, gain_k, clean, noise, grad_query, grad_key, grad_value,
    in_1, in_2, in_3, crossed, *refs
):
    out, cols = refs[-2:]
    f32 = jnp.float32
    keep, share = shares[0], shares[1]

    @pl.when(pl.program_id(0) == 0)
    def _():
        cols[...] = as_columns(rows_ref)

    clean_key = clean[1].astype(f32)
    noisy_query = keep * clean[0].astype(f32) + share * noise[0].astype(f32)
    noisy_key = keep * clean_key + share * noise[1].astype(f32)
    key_grad = crossed[0].astype(f32)
    value_grad = crossed[1].astype(f32)
    for hop, received in enumerate((in_1, in_2, in_3)):
        inside = flags[6 + hop] > 0
        key_grad = key_grad + jnp.where(inside, received[0], 0).astype(f32)
        value_grad = value_grad + jnp.where(inside, received[1], 0).astype(f32)
    col = lambda i: cols[:, i : i + 1]
    gk = gain_k[...]
    out[0] = keep * (col(0) * gain_q[...] * grad_query[...] - noisy_query * col(3))
    own = col(1) * gk * grad_key[...] - noisy_key * col(4)
    out[1] = keep * own + (col(2) * gk * key_grad - clean_key * col(5))
    out[2] = keep * grad_value[...] + value_grad


def finish_chunk(first, heads, flags, shares, factors, gains, fields, grads, received, crossed, previous):
    _, rows, width = fields[0].shape
    here = lambda h: (0, first + h)
    wide = pl.BlockSpec((rows, HEAD_DIM), here)
    gain_spec = pl.BlockSpec((1, HEAD_DIM), here)
    two = pl.BlockSpec((2, rows, HEAD_DIM), lambda h: (0, 0, first + h))
    pair = pl.BlockSpec((2, rows, HEAD_DIM), lambda h: (0, 0, h))
    smem = pl.BlockSpec(memory_space=pltpu.SMEM)
    operands = [flags, shares, factors, *gains, *fields, *grads, *received, crossed]
    in_specs = (
        [smem, smem, pl.BlockSpec((8, rows), lambda h: (0, 0))]
        + [gain_spec] * 2
        + [two] * 2
        + [wide] * 3
        + [pair] * 4
    )
    aliases = {}
    if previous is not None:
        aliases[len(operands)] = 0
        operands.append(previous)
        in_specs.append(pl.BlockSpec(memory_space=pl.ANY))
    return pl.pallas_call(
        finish_body,
        grid=(heads,),
        in_specs=in_specs,
        out_specs=pl.BlockSpec((3, rows, HEAD_DIM), lambda h: (0, 0, first + h)),
        out_shape=jax.ShapeDtypeStruct((3, rows, width), jnp.float32),
        scratch_shapes=[pltpu.VMEM((rows, HEAD_DIM), jnp.float32)],
        input_output_aliases=aliases,
        compiler_params=pltpu.CompilerParams(
            dimension_semantics=("arbitrary",), vmem_limit_bytes=VMEM_LIMIT
        ),
        cost_estimate=pl.CostEstimate(
            flops=rows * HEAD_DIM * heads * 30,
            bytes_accessed=heads * rows * HEAD_DIM * 48,
            transcendentals=0,
        ),
    )(*operands)


def head_sum(block):
    count = lax.axis_size("head")
    distance = 1
    while distance < count:
        route = [(i, i ^ distance) for i in range(count)]
        block = block + lax.ppermute(block, "head", route)
        distance *= 2
    return block


def after(value, *earlier):
    return lax.optimization_barrier((value, *earlier))[0]


def on_device(clean_qkv, noise_qkv, timestep, gain_q, gain_k, attended_grad):
    f32, bf16 = jnp.float32, jnp.bfloat16
    span = lax.axis_index("tm")
    column = span % COLUMNS
    steps = range(1, CONTEXT + 1)
    crossers = range(1, COLUMNS)
    value_clean = clean_qkv[2]

    def lanes(block, first, heads):
        return block[:, first * HEAD_DIM : (first + heads) * HEAD_DIM]

    def mixed(own, wrap):
        return [
            shift_columns(jnp.where(column + hop < COLUMNS, own, wrap), hop, "both")
            for hop in steps
        ]

    cross_values = shift_spans(value_clean, COLUMNS, crossers)
    first = [shift_columns(value_clean, hop, "inside") for hop in steps]

    noise_share = noise_share_of(timestep[0])
    shares = jnp.stack([1.0 - noise_share, noise_share])
    squares = prepare(shares, clean_qkv, noise_qkv)
    inverse = lax.rsqrt(head_sum(squares) / D + epsilon)
    key_clean = (clean_qkv[1].astype(f32) * inverse[2][:, None] * gain_k).astype(bf16)
    both = mixed(after(key_clean, *first), cross_values)
    cross_a = shift_spans(after(lanes(key_clean, 0, 2), cross_values), COLUMNS, crossers)
    cross_b = shift_spans(after(lanes(key_clean, 2, 3), cross_a), COLUMNS, crossers)
    last_a = [shift_columns(cross_a, hop, "wrapped") for hop in steps]
    last_b = [shift_columns(after(cross_b, *both), hop, "wrapped") for hop in steps]

    hops = jnp.arange(1, CONTEXT + 1, dtype=jnp.int32)
    flags = jnp.concatenate([column >= hops, span >= hops, column + hops < COLUMNS]).astype(
        jnp.int32
    )
    gains = (gain_q[None, :], gain_k[None, :])
    fields = (clean_qkv, noise_qkv)

    def attend(head, heads, last, last_at, spare, previous):
        out = attention_chunk(
            head, heads, flags, shares, inverse, gains, fields, attended_grad,
            (*first, *both), last, last_at, spare, previous,
        )
        return out[:4], out[4:7], out[7]

    def send_back(blocks):
        return [shift_columns(block, -hop, "both") for hop, block in zip(steps, blocks)]

    def cross_back(received):
        total = jnp.zeros(received[0].shape, f32)
        for hop, block in zip(steps, received):
            total = total + jnp.where(column + hop >= COLUMNS, block, 0).astype(f32)
        return shift_spans(total.astype(bf16), -COLUMNS, crossers)

    results, back, inner_0 = attend(0, 2, last_a, 0, 0, ())
    back_0 = send_back(back)
    crossed_0 = cross_back(back_0)
    results, kept, inner_1 = attend(2, 2, last_b, 0, 16, results)
    results, back, inner_2 = attend(4, 1, last_b, 2, 0, results)
    attended, *grads = results

    totals = head_sum(after(inner_0 + inner_1 + inner_2, *back_0)) / D
    high = lax.reduce_precision(totals[2:5], 8, 7)
    halves = jnp.stack([high, totals[2:5] - high]).reshape(2, CONTEXT, -1, 2 * HEAD_DIM)
    halves = jnp.pad(halves.astype(bf16), ((0, 0), (0, 0), (0, 14), (0, 0)))
    rows = attended_grad.shape[0]
    kept = [
        lax.dynamic_update_slice(block, halves[:, i], (0, rows, 0))
        for i, block in enumerate(kept)
    ]
    back_1 = send_back(after(tuple(kept), *back_0))
    crossed_1 = cross_back(back_1)
    back_2 = send_back(after(tuple(back), totals, crossed_0))
    crossed_2 = cross_back(back_2)

    def products_of(block):
        pieces = block[:, rows : rows + 2].astype(f32)
        return (pieces[0] + pieces[1]).reshape(-1)

    clean_inner = products_of(crossed_1)
    for hop, block in zip(steps, back_1):
        clean_inner = clean_inner + jnp.where(column + hop < COLUMNS, products_of(block), 0.0)
    cubes = jnp.stack(
        [
            inverse[0] ** 3 * totals[0],
            inverse[1] ** 3 * totals[1],
            inverse[2] ** 2 * clean_inner,
        ]
    )
    factors = jnp.concatenate([inverse[:3], cubes, cubes[:2]])
    clean_grads = None
    for head, heads, received, crossed in (
        (0, 2, back_0, crossed_0),
        (2, 2, back_1, crossed_1),
        (4, 1, back_2, crossed_2),
    ):
        clean_grads = finish_chunk(
            head, heads, flags, shares, factors, gains, fields, grads, received, crossed,
            clean_grads,
        )
    return (attended, clean_grads)


def solution(mesh):
    placed = (
        P(None, "tm", "head"),
        P(None, "tm", "head"),
        P("tm"),
        P("head"),
        P("head"),
        P("tm", "head"),
    )
    return jax.shard_map(
        on_device,
        mesh=mesh,
        in_specs=placed,
        out_specs=(P("tm", "head"), P(None, "tm", "head")),
        check_vma=False,
    )
```
